128 devices in a mesh: az: 8 (over y, z_lo), ta: 16 (over z_hi, x, core).
Axes of the slice: x: 4, y: 4, z: 4 (z_hi: 2, z_lo: 2; z = z_hi * 2 + z_lo), core: 2. Of those that a mesh axis runs over, the one named last changes fastest.
Arguments:
- initial_field: float32 [16, 2048, 8192], P(None, 'ta', 'az'), may hold values from -6 to 6
- conductivity: bfloat16 [16, 2048, 8192], P(None, 'ta', 'az'), may hold values from 0.25 to 4
- current_density: bfloat16 [16, 2048, 8192], P(None, 'ta', 'az'), may hold values from -6 to 6
- rotor_cycle: bfloat16 [2048, 8192], P('ta', 'az'), may hold values from -6 to 6
- skew_list: int32 [2048], P('ta'), may hold values from 0 to 63
Outputs:
- relaxed: float32 [16, 2048, 8192], P(None, 'ta', 'az')
The draws below stay inside these ranges and needn't reach their ends.
Inputs may be any that keep to these rules, and one draw needn't show every extreme that they name: `skew_list`: the rotor's offset in whole panels of 128 azimuth cells at each time step.
All inputs are finite; a program needn't handle non-finite values.
Results may differ from the reference program's by a relative error of at most 0.0003.
Values may be sent and summed in bfloat16 or wider, within the bound.
A program may use at most 192 MiB of HBM per device.

```python
import math
import jax
import jax.numpy as jnp
from jax import lax

R = 16
SWEEPS = 2
NA = 8192
NT = 2048
NPANELS = 64


def touch_ends(entries, key, smallest, largest):
    extent = entries.shape
    place = [jax.random.randint(jax.random.fold_in(key, axis), (), 0, extent[axis]) for axis in range(len(extent))]
    entries = entries.at[tuple(place)].set(smallest)
    longest = extent.index(max(extent))
    place[longest] = (place[longest] + 1) % extent[longest]
    return entries.at[tuple(place)].set(largest)


def block_levels(key, dims, shards, low, top_value):
    def one(axis_at, blocks):
        heights = jax.random.uniform(jax.random.fold_in(jax.random.fold_in(key, 6), axis_at), (blocks,), jnp.float32, low / len(shards), top_value / len(shards))
        return jnp.repeat(jnp.exp(heights), dims[axis_at] // blocks).reshape((-1,) + (1,) * (len(dims) - axis_at - 1))

    gain = one(*shards[0])
    for cut in shards[1:]:
        gain = gain * one(*cut)
    return gain


def gaussian(stream_key, extent, spread, bound, split=(), kind=jnp.bfloat16):
    gain = block_levels(stream_key, extent, split, -0.22, 0.18) if split else 1.0
    entries = jax.random.normal(stream_key, extent, jnp.float32) * spread * gain
    return jnp.minimum(jnp.maximum(entries, -bound), bound).astype(kind)


def setup_inputs(seed: int = 0) -> dict:
    arg_keys = jax.random.split(jax.random.key(seed), 6)
    initial_field = gaussian(arg_keys[0], (R, NT, NA), 1.0, 6.0, ((1, 16), (2, 8)), jnp.float32)
    conductivity = jnp.clip(jnp.exp(math.log(4.0) - 2.7725887 * jax.random.uniform(arg_keys[1], (R, NT, NA), jnp.float32) ** block_levels(arg_keys[1], (R, NT, NA), ((1, 16), (2, 8)), -0.2, 0.2)), 0.25, 4.0).astype(jnp.bfloat16)
    current_density = gaussian(arg_keys[2], (R, NT, NA), 1.0, 6.0, ((1, 16), (2, 8)))
    rotor_cycle = gaussian(arg_keys[3], (NT, NA), 1.0, 6.0, ((0, 16), (1, 8)))
    skew_list = touch_ends(jax.random.randint(arg_keys[4], (NT,), 0, NPANELS), jax.random.fold_in(arg_keys[4], 1), 0, NPANELS - 1).astype(jnp.int32)
    return {"initial_field": initial_field, "conductivity": conductivity, "current_density": current_density, "rotor_cycle": rotor_cycle, "skew_list": skew_list}


COEF_RADIAL = 1.0
COEF_AZIM = 1.0
COEF_TIME = 1.0 / 12.0
DIAGONAL = 4.0


def half_step(field_now, cycle_map, conductivity, current_density, colour):
    zero_layer = jnp.zeros((1, NT, NA), jnp.float32)
    stacked = jnp.concatenate([cycle_map.astype(jnp.float32)[None], field_now, zero_layer], 0)
    time_ids = jnp.arange(NT, dtype=jnp.int32)
    azim_ids = jnp.arange(NA, dtype=jnp.int32)
    plane_parity = time_ids[:, None] + azim_ids[None, :]

    def relax_layer(layer_no):
        middle = stacked[layer_no + 1]
        radial = stacked[layer_no] + stacked[layer_no + 2]
        azimuthal = jnp.roll(middle, 1, 1) + jnp.roll(middle, -1, 1)
        temporal = (-jnp.roll(middle, -2, 0) + 8.0 * jnp.roll(middle, -1, 0)
                    - 8.0 * jnp.roll(middle, 1, 0) + jnp.roll(middle, 2, 0))
        sigma = conductivity[layer_no].astype(jnp.float32)
        source = current_density[layer_no].astype(jnp.float32)
        update = (source + COEF_RADIAL * radial + COEF_AZIM * azimuthal - COEF_TIME * sigma * temporal) / DIAGONAL
        parity = jnp.remainder(plane_parity + layer_no, 2)
        return jnp.where(parity == colour, update, middle)

    return lax.map(relax_layer, jnp.arange(R, dtype=jnp.int32))


def reference(initial_field, conductivity, current_density, rotor_cycle, skew_list):
    columns = jnp.remainder(jnp.arange(NA, dtype=jnp.int32)[None, :] - 128 * skew_list[:, None], NA).astype(jnp.int32)
    cycle_map = jnp.take_along_axis(rotor_cycle, columns, axis=1)
    field_now = initial_field
    for sweep_no in range(SWEEPS):
        field_now = half_step(field_now, cycle_map, conductivity, current_density, 0)
        field_now = half_step(field_now, cycle_map, conductivity, current_density, 1)
    return field_now
```

```python
import jax, jax.numpy as jnp
from jax import lax
from jax.experimental import pallas as pl
from jax.experimental.pallas import tpu as pltpu
from jax.sharding import PartitionSpec as P

F32, BF16 = jnp.float32, jnp.bfloat16
MESH = pl.DeviceIdType.MESH
NAZ, NTA = 8, 16


def kernel_a(u_hbm, s_hbm, c_hbm, rot_hbm, sk, hu, hs, hc, m, mh, cyc, cych,
             eu, es16, ec16, es, ec, su, ss, sc, cu, cs, cc, pu, ps, pc, qu, qs, qc, w0, w1, v,
             edge_sem, col_sem, own_sem, p1s, p1r, p3s, p3r, azs, azr, tas, tar, cos, cor, cys, cyr):
    az, ta = lax.axis_index("az"), lax.axis_index("ta")
    up, down = lax.rem(ta + NTA - 1, NTA), lax.rem(ta + 1, NTA)
    left, right = lax.rem(az + NAZ - 1, NAZ), lax.rem(az + 1, NAZ)
    others = [lax.rem(az + o, NAZ) for o in range(1, NAZ)]

    edges = []
    for q, (h, e) in enumerate(((u_hbm, eu), (s_hbm, es16), (c_hbm, ec16))):
        for side, t in ((0, 120), (1, 0)):
            for j in range(8):
                edges.append(pltpu.make_async_copy(h.at[:, pl.ds(t, 8), pl.ds(128 * j, 128)], e.at[side, j],
                                                   edge_sem.at[q, side, j]))
    cols = []
    for q, (h, e) in enumerate(((u_hbm, cu), (s_hbm, cs), (c_hbm, cc))):
        for side, n in ((0, 0), (1, 896)):
            cols.append(pltpu.make_async_copy(h.at[:, :, pl.ds(n, 128)], e.at[side], col_sem.at[q, side]))
    barrier = pltpu.get_barrier_semaphore()
    for d in others:
        pl.semaphore_signal(barrier, inc=1, device_id={"az": d}, device_id_type=MESH)
    for d in (up, down):
        pl.semaphore_signal(barrier, inc=1, device_id={"ta": d}, device_id_type=MESH)
    for c in edges: c.start()
    own = pltpu.make_async_copy(rot_hbm.at[pl.ds(16 * az, 16), :], w0.at[:, pl.ds(1024 * az, 1024)], own_sem.at[0])
    own.start()
    for c in cols: c.start()
    pl.semaphore_wait(barrier, NAZ + 1)

    first = []
    for o, d in enumerate(others):
        first.append(pltpu.make_async_remote_copy(
            src_ref=rot_hbm.at[pl.ds(16 * d, 16), :], dst_ref=w0.at[:, pl.ds(1024 * az, 1024)],
            send_sem=p1s.at[o], recv_sem=p1r.at[o], device_id={"az": d}, device_id_type=MESH))
    for c in first: c.start()

    lane = lax.broadcasted_iota(jnp.int32, (8, 128), 1)
    rowi = lax.broadcasted_iota(jnp.int32, (8, 128), 0)
    odd_lane = (lane & 1) == 1
    odd = ((lane + rowi) & 1) == 1
    for c in edges: c.wait()

    def widen(i, _):
        for side in range(2):
            for j in range(8):
                es[side, j, i] = es16[side, j, i].astype(F32)
                ec[side, j, i] = ec16[side, j, i].astype(F32)
        return 0
    lax.fori_loop(0, 16, widen, 0)
    flat = [e.reshape(2 * 8 * 16 * 8, 128) for e in (eu, es, ec)]

    def pairs(q, side, j, s, colour):
        base = (side * 8 + j) * 128 + s
        even, odd_layer = flat[q][pl.ds(base, 8, stride=16), :], flat[q][pl.ds(base + 8, 8, stride=16), :]
        return jnp.where(odd_lane, odd_layer, even) if (s + colour) % 2 == 0 else jnp.where(odd_lane, even, odd_layer)

    for side in range(2):
        for j in range(8):
            ln = slice(128 * j, 128 * j + 128)
            reds = (3, 4, 5, 6, 7) if side == 0 else (0, 1, 2, 3, 4)
            blacks = (4, 5, 6, 7) if side == 0 else (0, 1, 2, 3)
            for i, s in enumerate(reds):
                su[side, i, :, ln] = pairs(0, side, j, s, 0)
            for i, s in enumerate(blacks):
                su[side, 5 + i, :, ln] = pairs(0, side, j, s, 1)
            for i, (s, c) in enumerate(((5, 0), (6, 0), (7, 0), (6, 1), (7, 1)) if side == 0 else
                                       ((0, 0), (1, 0), (2, 0), (0, 1), (1, 1))):
                ss[side, i, :, ln] = pairs(1, side, j, s, c).astype(BF16)
                sc[side, i, :, ln] = pairs(2, side, j, s, c).astype(BF16)
    second = []
    for side, d in ((0, down), (1, up)):
        for q, (a, b) in enumerate(((su, hu), (ss, hs), (sc, hc))):
            second.append(pltpu.make_async_remote_copy(
                src_ref=a.at[side], dst_ref=b.at[side], send_sem=tas.at[side, q], recv_sem=tar.at[side, q],
                device_id={"ta": d}, device_id_type=MESH))
    for c in second: c.start()

    for c in cols: c.wait()
    lane16 = lax.broadcasted_iota(jnp.int32, (16, 128), 1)
    row16 = lax.broadcasted_iota(jnp.int32, (16, 128), 0)
    odd16 = ((lane16 + row16) & 1) == 1
    low = lane16 < 64

    def columns(i, _):
        rows = pl.ds(pl.multiple_of(16 * i, 16), 16)
        for src, dst in ((cu, pu), (cs, ps), (cc, pc)):
            acc = jnp.zeros((16, 128), F32)
            for k in range(8):
                even = jnp.where(low, src[0, 2 * k, rows, :].astype(F32), src[1, 2 * k, rows, :].astype(F32))
                odd_l = jnp.where(low, src[0, 2 * k + 1, rows, :].astype(F32), src[1, 2 * k + 1, rows, :].astype(F32))
                red, black = jnp.where(odd16, odd_l, even), jnp.where(odd16, even, odd_l)
                for a, x in ((k, red), (k + 8, black)):
                    acc = jnp.where((lane16 >> 3) == a, pltpu.roll(x, (8 * a + 4) % 128, 1), acc)
            dst[rows, :] = acc.astype(dst.dtype)
        return 0
    lax.fori_loop(0, 8, columns, 0)
    third = []
    for side, d in ((0, right), (1, left)):
        for q, (a, b) in enumerate(((pu, qu), (ps, qs), (pc, qc))):
            third.append(pltpu.make_async_remote_copy(
                src_ref=a, dst_ref=b.at[side], send_sem=azs.at[side, q], recv_sem=azr.at[side, q],
                device_id={"az": d}, device_id_type=MESH))
    for c in third: c.start()

    own.wait()
    for c in first: c.wait_recv()
    amount = sk[pl.ds(pl.multiple_of(16 * az, 16), 16), :]
    src, dst = w0, w1
    for b in range(6):
        bit = ((amount >> b) & 1) == 1
        for p in range(64):
            f = (p - (1 << b)) % 64
            dst[:, 128 * p:128 * p + 128] = jnp.where(bit, src[:, 128 * f:128 * f + 128], src[:, 128 * p:128 * p + 128])
        src, dst = dst, src
    for d in range(8):
        for jj in range(8):
            v[d, jj] = w0[:, 1024 * d + 128 * jj:1024 * d + 128 * jj + 128]
        after, before = (8 * d + 8) % 64, (8 * d - 1) % 64
        v[d, 8] = jnp.where(low, w0[:, 128 * after:128 * after + 128], w0[:, 128 * before:128 * before + 128])
    rows = pl.ds(16 * az, 16)
    mine = pltpu.make_async_copy(v.at[az], cyc.at[:, rows, :], own_sem.at[1])
    mine.start()
    fourth = []
    for o, d in enumerate(others):
        fourth.append(pltpu.make_async_remote_copy(
            src_ref=v.at[d], dst_ref=cyc.at[:, rows, :], send_sem=p3s.at[o], recv_sem=p3r.at[o],
            device_id={"az": d}, device_id_type=MESH))
    for c in fourth: c.start()

    for c in third: c.wait_recv()
    from_left = (lane16 & 7) < 4

    def merge(i, _):
        rr = pl.ds(pl.multiple_of(16 * i, 16), 16)
        for q, b in enumerate((qu, qs, qc)):
            m[q, rr, :] = jnp.where(from_left, b[0, rr, :].astype(F32), b[1, rr, :].astype(F32))
        return 0
    lax.fori_loop(0, 8, merge, 0)
    fifth = []
    for side, d, t in ((0, down, 120), (1, up, 0)):
        fifth.append(pltpu.make_async_remote_copy(
            src_ref=m.at[:, pl.ds(t, 8), :], dst_ref=mh.at[side], send_sem=cos.at[side], recv_sem=cor.at[side],
            device_id={"ta": d}, device_id_type=MESH))
    for c in fifth: c.start()

    mine.wait()
    for c in fourth: c.wait_recv()
    sixth = []
    for side, d, t in ((0, down, 112), (1, up, 0)):
        sixth.append(pltpu.make_async_remote_copy(
            src_ref=cyc.at[:, pl.ds(t, 16), :], dst_ref=cych.at[side], send_sem=cys.at[side], recv_sem=cyr.at[side],
            device_id={"ta": d}, device_id_type=MESH))
    for c in sixth: c.start()
    for c in first + third + fourth: c.wait_send()
    for c in second + fifth + sixth: c.wait()


def call_a(u, s, c, rot, skew):
    sk = jnp.broadcast_to(skew[:, None], (128, 128))
    anys = pl.BlockSpec(memory_space=pl.ANY)
    vm = pl.BlockSpec(memory_space=pltpu.VMEM)
    D = pltpu.SemaphoreType.DMA
    return pl.pallas_call(
        kernel_a,
        out_shape=(jax.ShapeDtypeStruct((2, 9, 8, 1024), F32), jax.ShapeDtypeStruct((2, 5, 8, 1024), BF16),
                   jax.ShapeDtypeStruct((2, 5, 8, 1024), BF16), jax.ShapeDtypeStruct((3, 128, 128), F32),
                   jax.ShapeDtypeStruct((2, 3, 8, 128), F32), jax.ShapeDtypeStruct((9, 128, 128), BF16),
                   jax.ShapeDtypeStruct((2, 9, 16, 128), BF16)),
        in_specs=[anys] * 4 + [vm],
        out_specs=(anys, anys, anys, vm, anys, anys, anys),
        scratch_shapes=[pltpu.VMEM((2, 8, 16, 8, 128), F32), pltpu.VMEM((2, 8, 16, 8, 128), BF16), pltpu.VMEM((2, 8, 16, 8, 128), BF16),
                        pltpu.VMEM((2, 8, 16, 8, 128), F32), pltpu.VMEM((2, 8, 16, 8, 128), F32),
                        pltpu.VMEM((2, 9, 8, 1024), F32), pltpu.VMEM((2, 5, 8, 1024), BF16), pltpu.VMEM((2, 5, 8, 1024), BF16),
                        pltpu.VMEM((2, 16, 128, 128), F32), pltpu.VMEM((2, 16, 128, 128), BF16), pltpu.VMEM((2, 16, 128, 128), BF16),
                        pltpu.VMEM((128, 128), F32), pltpu.VMEM((128, 128), BF16), pltpu.VMEM((128, 128), BF16),
                        pltpu.VMEM((2, 128, 128), F32), pltpu.VMEM((2, 128, 128), BF16), pltpu.VMEM((2, 128, 128), BF16),
                        pltpu.VMEM((16, 8192), BF16), pltpu.VMEM((16, 8192), BF16), pltpu.VMEM((8, 9, 16, 128), BF16),
                        D((3, 2, 8)), D((3, 2)), D((2,)), D((7,)), D((7,)), D((7,)), D((7,)), D((2, 3)), D((2, 3)), D((2, 3)), D((2, 3)),
                        D((2,)), D((2,)), D((2,)), D((2,))],
        compiler_params=pltpu.CompilerParams(collective_id=0, has_side_effects=True, vmem_limit_bytes=40000 * 1024),
        name="exchange",
    )(u, s, c, rot, sk)


NK, NJ, ROWS, T0 = 8, 9, 152, 12
PITCH = NJ * ROWS


def kernel_b(u_hbm, s_hbm, c_hbm, hu_hbm, hs_hbm, hc_hbm, m_hbm, mh_hbm, cyc_hbm, cych_hbm, out_hbm,
             r_a, r_b, b_a, b_b, sg, jg, us, ss, cs, outs, hu, hs, hc, m, mh, cyc, cych,
             in_sem, out_sem, aux_sem):
    rowi = lax.broadcasted_iota(jnp.int32, (8, 128), 0)
    lane = lax.broadcasted_iota(jnp.int32, (8, 128), 1)
    odd = ((rowi + lane) & 1) == 1
    odd_lane = (lane & 1) == 1
    first = lane == 0
    last = lane == 127

    def in_copies(k, slot):
        pair = pl.ds(2 * k, 2)
        return [pltpu.make_async_copy(h.at[pair], v.at[slot], in_sem.at[i, slot])
                for i, (h, v) in enumerate(((u_hbm, us), (s_hbm, ss), (c_hbm, cs)))]

    def out_copy(k, slot):
        return pltpu.make_async_copy(outs.at[slot], out_hbm.at[pl.ds(2 * k, 2)], out_sem.at[slot])

    aux = [pltpu.make_async_copy(a, b, aux_sem.at[i]) for i, (a, b) in enumerate(
        ((hu_hbm, hu), (hs_hbm, hs), (hc_hbm, hc), (m_hbm, m), (mh_hbm, mh), (cyc_hbm, cyc), (cych_hbm, cych)))]
    for c in in_copies(NK - 1, 0): c.start()
    for c in aux: c.start()
    for c in in_copies(NK - 2, 1): c.start()

    def row(kk, j, rho):
        return kk * PITCH + j * ROWS + rho

    zero = jnp.zeros((8, 128), F32)
    for j in range(NJ):
        for i in range(ROWS // 8):
            for ref in (r_a, r_b, b_a, b_b):
                ref[pl.ds(row(NK + 1, j, 8 * i), 8), :] = zero
    for c in aux: c.wait()
    for j in range(NJ):
        for i in range(8):
            x = cyc[j, 16 * i:16 * i + 16, :].astype(F32)
            for ref in (r_a, r_b, b_a, b_b):
                ref[pl.ds(row(0, j, T0 + 16 * i), 16), :] = x
        top = cych[0, j].astype(F32)[8:]
        bot = cych[1, j].astype(F32)[:8]
        for ref in (r_a, r_b, b_a, b_b):
            ref[pl.ds(row(0, j, T0 - 8), 8), :] = top
            ref[pl.ds(row(0, j, T0 + 128), 8), :] = bot

    def spread(ref, base, j, t, tile):
        ref[pl.ds(base + j * ROWS + T0 + t, NK, stride=PITCH), :] = tile

    for j in range(8):
        cols = slice(128 * j, 128 * j + 128)
        for side in range(2):
            for i in range(5):
                spread(r_a, PITCH, j, (-5 if side == 0 else 128) + i, hu[side, i, :, cols])
            for i in range(4):
                spread(b_a, PITCH, j, (-4 if side == 0 else 128) + i, hu[side, 5 + i, :, cols])
            for i in range(5):
                t = ((-3, -2, -1, -2, -1) if side == 0 else (128, 129, 130, 128, 129))[i]
                base = 0 if i < 3 else NK * PITCH
                spread(sg, base, j, t, hs[side, i, :, cols].astype(F32) * (1.0 / 48.0))
                spread(jg, base, j, t, hc[side, i, :, cols].astype(F32))

    for i in range(18):
        for q in range(3):
            if i == 0:
                src, rho = mh[0, q], T0 - 8
            elif i == 17:
                src, rho = mh[1, q], T0 + 128
            else:
                src, rho = m[q, 8 * (i - 1):8 * i, :], T0 + 8 * (i - 1)
            if q == 1:
                src = src * (1.0 / 48.0)
            for a in range(16):
                x = pltpu.roll(src, (124 - 8 * a) % 128, 1)
                if q == 0:
                    (r_a if a < 8 else b_a)[pl.ds(row(a % 8 + 1, NJ - 1, rho), 8), :] = x
                else:
                    (sg if q == 1 else jg)[pl.ds(a * PITCH + (NJ - 1) * ROWS + rho, 8), :] = x

    def pack(k, slot):
        st = (k + 1) * PITCH
        c0, c1 = k * PITCH, (k + NK) * PITCH
        for i in range(8):
            rows = slice(16 * i, 16 * i + 16)
            for j in range(8):
                cols = slice(128 * j, 128 * j + 128)
                for h in range(2):
                    r8 = slice(16 * i + 8 * h, 16 * i + 8 * h + 8)
                    dst = j * ROWS + T0 + 16 * i + 8 * h
                    e, o = us[slot, 0, r8, cols], us[slot, 1, r8, cols]
                    r_a[pl.ds(st + dst, 8), :] = jnp.where(odd, o, e)
                    b_a[pl.ds(st + dst, 8), :] = jnp.where(odd, e, o)
                e16, o16 = ss[slot, 0, rows, cols].astype(F32) * (1.0 / 48.0), ss[slot, 1, rows, cols].astype(F32) * (1.0 / 48.0)
                f16, p16 = cs[slot, 0, rows, cols].astype(F32), cs[slot, 1, rows, cols].astype(F32)
                for h in range(2):
                    dst = j * ROWS + T0 + 16 * i + 8 * h
                    e, o = e16[8 * h:8 * h + 8], o16[8 * h:8 * h + 8]
                    sg[pl.ds(c0 + dst, 8), :] = jnp.where(odd, o, e)
                    sg[pl.ds(c1 + dst, 8), :] = jnp.where(odd, e, o)
                    e, o = f16[8 * h:8 * h + 8], p16[8 * h:8 * h + 8]
                    jg[pl.ds(c0 + dst, 8), :] = jnp.where(odd, o, e)
                    jg[pl.ds(c1 + dst, 8), :] = jnp.where(odd, e, o)

    def half(k, colour, src, own, rho, nj, emit):
        st = (k + 1) * PITCH
        co = (k + colour * NK) * PITCH
        cen = [src[pl.ds(st + j * ROWS + rho, 8), :] for j in range(NJ)]
        rl = [pltpu.roll(x, 1, 1) for x in cen]
        rr = [pltpu.roll(x, 127, 1) for x in cen]
        for j in range(nj):
            off = j * ROWS + rho
            left = jnp.where(first, rl[(j - 1) % NJ], rl[j])
            right = jnp.where(last, rr[(j + 1) % NJ], rr[j])
            lo, hi = src[pl.ds(st - PITCH + off, 8), :], src[pl.ds(st + PITCH + off, 8), :]
            rad = jnp.where(odd, hi, lo) if colour == 0 else jnp.where(odd, lo, hi)
            d1 = src[pl.ds(st + off + 1, 8), :] - src[pl.ds(st + off - 1, 8), :]
            d2 = own[pl.ds(st + off + 2, 8), :] - own[pl.ds(st + off - 2, 8), :]
            acc = ((jg[pl.ds(co + off, 8), :] + rad) + cen[j]) + (left + right)
            emit(j, rho, acc * 0.25 - sg[pl.ds(co + off, 8), :] * (d1 * 8.0 - d2))

    def unit(k, colour, src, own, dst):
        st = (k + 1) * PITCH
        def emit(j, rho, val):
            dst[pl.ds(st + j * ROWS + rho, 8), :] = val
        for i in range(17):
            half(k, colour, src, own, 8 + 8 * i, NJ, emit)

    def final(k, slot):
        st = (k + 1) * PITCH
        def emit(j, rho, val):
            red = r_a[pl.ds(st + j * ROWS + rho, 8), :]
            t = rho - T0
            outs[slot, 0, t:t + 8, 128 * j:128 * j + 128] = jnp.where(odd, val, red)
            outs[slot, 1, t:t + 8, 128 * j:128 * j + 128] = jnp.where(odd, red, val)
        for i in range(16):
            half(k, 1, r_a, b_b, T0 + 8 * i, 8, emit)

    def step(s, _):
        @pl.when(s < NK)
        def _():
            k = NK - 1 - s
            slot = lax.rem(s, 2)
            for c in in_copies(k, slot): c.wait()
            pack(k, slot)
            @pl.when(s + 2 < NK)
            def _():
                for c in in_copies(k - 2, slot): c.start()
        @pl.when((s >= 1) & (s < NK + 1))
        def _():
            unit(NK - s, 0, b_a, r_a, r_b)
        @pl.when((s >= 2) & (s < NK + 2))
        def _():
            unit(NK + 1 - s, 1, r_b, b_a, b_b)
        @pl.when((s >= 3) & (s < NK + 3))
        def _():
            unit(NK + 2 - s, 0, b_b, r_b, r_a)
        @pl.when(s >= 4)
        def _():
            k = NK + 3 - s
            slot = lax.rem(s, 2)
            @pl.when(s >= 6)
            def _():
                out_copy(k + 2, slot).wait()
            final(k, slot)
            out_copy(k, slot).start()
        return 0
    lax.fori_loop(0, NK + 4, step, 0)
    out_copy(1, 0).wait()
    out_copy(0, 1).wait()


def call_b(*args):
    state = pltpu.VMEM(((NK + 2) * PITCH, 128), F32)
    coef = pltpu.VMEM((2 * NK * PITCH, 128), F32)
    return pl.pallas_call(
        kernel_b,
        out_shape=jax.ShapeDtypeStruct((16, 128, 1024), F32),
        in_specs=[pl.BlockSpec(memory_space=pl.ANY)] * 10,
        out_specs=pl.BlockSpec(memory_space=pl.ANY),
        scratch_shapes=[state, state, state, state, coef, coef,
                        pltpu.VMEM((2, 2, 128, 1024), F32), pltpu.VMEM((2, 2, 128, 1024), BF16),
                        pltpu.VMEM((2, 2, 128, 1024), BF16), pltpu.VMEM((2, 2, 128, 1024), F32),
                        pltpu.VMEM((2, 9, 8, 1024), F32), pltpu.VMEM((2, 5, 8, 1024), BF16), pltpu.VMEM((2, 5, 8, 1024), BF16),
                        pltpu.VMEM((3, 128, 128), F32), pltpu.VMEM((2, 3, 8, 128), F32),
                        pltpu.VMEM((9, 128, 128), BF16), pltpu.VMEM((2, 9, 16, 128), BF16),
                        pltpu.SemaphoreType.DMA((3, 2)), pltpu.SemaphoreType.DMA((2,)), pltpu.SemaphoreType.DMA((7,))],
        compiler_params=pltpu.CompilerParams(vmem_limit_bytes=65400 * 1024),
        name="relax",
    )(*args)


def local(u, s, c, rot, skew):
    return call_b(u, s, c, *call_a(u, s, c, rot, skew))


def solution(mesh):
    placed = (P(None, "ta", "az"), P(None, "ta", "az"), P(None, "ta", "az"), P("ta", "az"), P("ta"))
    return jax.shard_map(
        local, mesh=mesh, in_specs=placed, out_specs=P(None, "ta", "az"), check_vma=False
    )
```

```python
import jax
import jax.numpy as jnp
from jax import lax
from jax.experimental import pallas as pl
from jax.experimental.pallas import tpu as pltpu
from jax.sharding import PartitionSpec as P

F32, BF16 = jnp.float32, jnp.bfloat16
MESH = pl.DeviceIdType.MESH
NAZ, NTA = 8, 16
NK, NJ, ROWS, T0 = 8, 9, 152, 12
PITCH = NJ * ROWS
SIXTY = 1.0 / 48.0
LIMIT = 29700 * 1024
LIMIT2 = 29700 * 1024
RED_ROWS = ((3, 4, 5, 6, 7), (0, 1, 2, 3, 4))
BLACK_ROWS = ((4, 5, 6, 7), (0, 1, 2, 3))
COEF_ROWS = (((5, 0), (6, 0), (7, 0), (6, 1), (7, 1)), ((0, 0), (1, 0), (2, 0), (0, 1), (1, 1)))


def row(kk, j, rho):
    return kk * PITCH + j * ROWS + rho


def exchange(u_hbm, s_hbm, c_hbm, rot_hbm, sk, r_a, b_a, sg, jg,
             us, ss, cs, eu, es, ec, er, su, ts, tc, hu, hs, hc, ku, ks, kc, pu, ps, pc, pd, qu, qs, qc, qd,
             w0, w1, v, cyc, cych,
             in_sem, edge_sem, col_sem, own_sem, p1s, p1r, p3s, p3r, azs, azr, tas, tar, dis, dir_, cys, cyr):
    az, ta = lax.axis_index("az"), lax.axis_index("ta")
    up, down = lax.rem(ta + NTA - 1, NTA), lax.rem(ta + 1, NTA)
    left_az, right_az = lax.rem(az + NAZ - 1, NAZ), lax.rem(az + 1, NAZ)
    others = [lax.rem(az + o, NAZ) for o in range(1, NAZ)]
    diagonals = [(side, other, t, a) for side, t in ((0, down), (1, up)) for other, a in ((0, right_az), (1, left_az))]

    rowi = lax.broadcasted_iota(jnp.int32, (8, 128), 0)
    lane = lax.broadcasted_iota(jnp.int32, (8, 128), 1)
    odd = ((rowi + lane) & 1) == 1
    lane16 = lax.broadcasted_iota(jnp.int32, (16, 128), 1)
    row16 = lax.broadcasted_iota(jnp.int32, (16, 128), 0)
    odd16 = ((lane16 + row16) & 1) == 1
    low16 = lane16 < 64

    def remote(src, dst, ssem, rsem, dev):
        return pltpu.make_async_remote_copy(src_ref=src, dst_ref=dst, send_sem=ssem, recv_sem=rsem,
                                            device_id=dev, device_id_type=MESH)

    def in_copies(k, slot):
        pair = pl.ds(2 * k, 2)
        return [pltpu.make_async_copy(h.at[pair], dst.at[slot], in_sem.at[i, slot])
                for i, (h, dst) in enumerate(((u_hbm, us), (s_hbm, ss), (c_hbm, cs)))]

    edges = [pltpu.make_async_copy(h.at[:, pl.ds(t, 8), :], e.at[side], edge_sem.at[q, side])
             for q, (h, e) in enumerate(((u_hbm, eu), (s_hbm, es), (c_hbm, ec))) for side, t in ((0, 120), (1, 0))]
    cols = [pltpu.make_async_copy(h.at[:, :, pl.ds(n, 128)], e.at[side], col_sem.at[q, side])
            for q, (h, e) in enumerate(((u_hbm, ku), (s_hbm, ks), (c_hbm, kc))) for side, n in ((0, 0), (1, 896))]

    barrier = pltpu.get_barrier_semaphore()
    for d in others:
        pl.semaphore_signal(barrier, inc=1, device_id={"az": d}, device_id_type=MESH)
    for t in (up, down):
        for a in range(NAZ):
            pl.semaphore_signal(barrier, inc=1, device_id={"ta": t, "az": a}, device_id_type=MESH)
    for c in edges: c.start()
    for c in cols: c.start()
    own = pltpu.make_async_copy(rot_hbm.at[pl.ds(16 * az, 16), :], w0.at[:, pl.ds(1024 * az, 1024)], own_sem.at[0])
    own.start()
    for c in in_copies(NK - 1, 0): c.start()
    for c in in_copies(NK - 2, 1): c.start()
    pl.semaphore_wait(barrier, 3 * NAZ - 1)
    first_hop = [remote(rot_hbm.at[pl.ds(16 * d, 16), :], w0.at[:, pl.ds(1024 * az, 1024)], p1s.at[o], p1r.at[o], {"az": d})
                 for o, d in enumerate(others)]
    for c in first_hop: c.start()

    for c in edges: c.wait()
    for side in range(2):
        for q, e in enumerate((eu, es, ec)):
            for j in range(8):
                ln = slice(128 * j, 128 * j + 128)
                base = ((q * 2 + side) * 8 + j) * 128
                for k in range(NK):
                    even, odd_layer = e[side, 2 * k, :, ln].astype(F32), e[side, 2 * k + 1, :, ln].astype(F32)
                    er[base + 8 * k:base + 8 * k + 8, :] = jnp.where(odd, odd_layer, even)
                    er[base + 64 + 8 * k:base + 72 + 8 * k, :] = jnp.where(odd, even, odd_layer)
                if q == 0:
                    for i, t in enumerate(RED_ROWS[side]):
                        su[side, i, :, ln] = er[pl.ds(base + t, NK, stride=8), :]
                    for i, t in enumerate(BLACK_ROWS[side]):
                        su[side, 5 + i, :, ln] = er[pl.ds(base + 64 + t, NK, stride=8), :]
                else:
                    for i, (t, colour) in enumerate(COEF_ROWS[side]):
                        (ts if q == 1 else tc)[side, i, :, ln] = er[pl.ds(base + 64 * colour + t, NK, stride=8), :].astype(BF16)
    time_hop = [remote(a.at[side], b.at[side], tas.at[side, q], tar.at[side, q], {"ta": d})
                for side, d in ((0, down), (1, up)) for q, (a, b) in enumerate(((su, hu), (ts, hs), (tc, hc)))]
    for c in time_hop: c.start()

    for c in cols: c.wait()

    def columns(i, _):
        rows = pl.ds(pl.multiple_of(16 * i, 16), 16)
        for src, dst in ((ku, pu), (ks, ps), (kc, pc)):
            acc = jnp.zeros((16, 128), F32)
            for k in range(NK):
                even = jnp.where(low16, src[0, 2 * k, rows, :].astype(F32), src[1, 2 * k, rows, :].astype(F32))
                odd_l = jnp.where(low16, src[0, 2 * k + 1, rows, :].astype(F32), src[1, 2 * k + 1, rows, :].astype(F32))
                red, black = jnp.where(odd16, odd_l, even), jnp.where(odd16, even, odd_l)
                for a, x in ((k, red), (k + 8, black)):
                    acc = jnp.where((lane16 >> 3) == a, pltpu.roll(x, (8 * a + 4) % 128, 1), acc)
            dst[rows, :] = acc.astype(dst.dtype)
        return 0
    lax.fori_loop(0, 8, columns, 0)
    for q, src in enumerate((pu, ps, pc)):
        pd[0, q] = src[112:128, :].astype(F32)[8:]
        pd[1, q] = src[0:16, :].astype(F32)[:8]
    az_hop = [remote(a, b.at[side], azs.at[side, q], azr.at[side, q], {"az": d})
              for side, d in ((0, right_az), (1, left_az)) for q, (a, b) in enumerate(((pu, qu), (ps, qs), (pc, qc)))]
    diag_hop = [remote(pd.at[side], qd.at[side, other], dis.at[side, other], dir_.at[side, other], {"ta": t, "az": a})
                for side, other, t, a in diagonals]
    for c in az_hop + diag_hop: c.start()

    def pack(s, _):
        k = NK - 1 - s
        slot = lax.rem(s, 2)
        for c in in_copies(k, slot): c.wait()
        st, c0, c1 = (k + 1) * PITCH, k * PITCH, (k + NK) * PITCH
        for i in range(8):
            rows = slice(16 * i, 16 * i + 16)
            for j in range(8):
                ln = slice(128 * j, 128 * j + 128)
                e16, o16 = ss[slot, 0, rows, ln].astype(F32) * SIXTY, ss[slot, 1, rows, ln].astype(F32) * SIXTY
                f16, p16 = cs[slot, 0, rows, ln].astype(F32), cs[slot, 1, rows, ln].astype(F32)
                for h in range(2):
                    part, r8 = slice(8 * h, 8 * h + 8), slice(16 * i + 8 * h, 16 * i + 8 * h + 8)
                    at = j * ROWS + T0 + 16 * i + 8 * h
                    for e, o, ra, rb, pa, pb in ((us[slot, 0, r8, ln], us[slot, 1, r8, ln], r_a, b_a, st, st),
                                                 (e16[part], o16[part], sg, sg, c0, c1), (f16[part], p16[part], jg, jg, c0, c1)):
                        ra[pl.ds(pa + at, 8), :] = jnp.where(odd, o, e)
                        rb[pl.ds(pb + at, 8), :] = jnp.where(odd, e, o)

        @pl.when(s + 2 < NK)
        def _():
            for c in in_copies(k - 2, slot): c.start()
        return 0

    own.wait()
    for c in first_hop: c.wait_recv()
    amount = sk[pl.ds(pl.multiple_of(16 * az, 16), 16), :]
    src, dst = w0, w1
    for b in range(6):
        bit = ((amount >> b) & 1) == 1
        for p in range(64):
            f = (p - (1 << b)) % 64
            dst[:, 128 * p:128 * p + 128] = jnp.where(bit, src[:, 128 * f:128 * f + 128], src[:, 128 * p:128 * p + 128])
        src, dst = dst, src
    for d in range(NAZ):
        for jj in range(8):
            v[d, jj] = w0[:, 1024 * d + 128 * jj:1024 * d + 128 * jj + 128]
        after, before = (8 * d + 8) % 64, (8 * d - 1) % 64
        v[d, 8] = jnp.where(low16, w0[:, 128 * after:128 * after + 128], w0[:, 128 * before:128 * before + 128])
    block = pl.ds(16 * az, 16)
    mine = pltpu.make_async_copy(v.at[az], cyc.at[:, block, :], own_sem.at[1])
    mine.start()
    second_hop = [remote(v.at[d], cyc.at[:, block, :], p3s.at[o], p3r.at[o], {"az": d}) for o, d in enumerate(others)]
    for c in second_hop: c.start()
    beyond = [[remote(v.at[d], cych.at[side], cys.at[d], cyr.at[side], {"ta": t, "az": d}) for d in range(NAZ)]
              for side, t in ((0, down), (1, up))]

    @pl.when(az == NAZ - 1)
    def _():
        for c in beyond[0]: c.start()

    @pl.when(az == 0)
    def _():
        for c in beyond[1]: c.start()

    lax.fori_loop(0, NK, pack, 0)

    zero = jnp.zeros((8, 128), F32)
    for j in range(NJ):
        for i in range(ROWS // 8):
            for ref in (r_a, b_a):
                ref[pl.ds(row(NK + 1, j, 8 * i), 8), :] = zero

    for c in az_hop: c.wait_recv()
    for c in diag_hop: c.wait_recv()
    mine_lane = (lane & 7) < 4
    mine16 = (lane16 & 7) < 4

    def place(q, x, rho):
        if q == 1:
            x = x * SIXTY
        for a in range(16):
            y = pltpu.roll(x, (124 - 8 * a) % 128, 1)
            if q == 0:
                (r_a if a < 8 else b_a)[pl.ds(row(a % 8 + 1, NJ - 1, rho), 8), :] = y
            else:
                (sg if q == 1 else jg)[pl.ds(a * PITCH + (NJ - 1) * ROWS + rho, 8), :] = y

    for q, b in enumerate((qu, qs, qc)):
        for side, rho in ((0, T0 - 8), (1, T0 + 128)):
            place(q, jnp.where(mine_lane, qd[side, 0, q], qd[side, 1, q]), rho)
        for i in range(8):
            x = jnp.where(mine16, b[0, 16 * i:16 * i + 16, :].astype(F32), b[1, 16 * i:16 * i + 16, :].astype(F32))
            for h in range(2):
                place(q, x[8 * h:8 * h + 8], T0 + 16 * i + 8 * h)

    mine.wait()
    for c in second_hop: c.wait_recv()
    for side in range(2): beyond[side][0].wait_recv()
    for j in range(NJ):
        for i in range(8):
            x = cyc[j, 16 * i:16 * i + 16, :].astype(F32)
            for ref in (r_a, b_a):
                ref[pl.ds(row(0, j, T0 + 16 * i), 16), :] = x
        top, bottom = cych[0, j].astype(F32)[8:], cych[1, j].astype(F32)[:8]
        for ref in (r_a, b_a):
            ref[pl.ds(row(0, j, T0 - 8), 8), :] = top
            ref[pl.ds(row(0, j, T0 + 128), 8), :] = bottom

    for c in time_hop: c.wait_recv()

    def spread(ref, base, j, t, tile):
        ref[pl.ds(base + j * ROWS + T0 + t, NK, stride=PITCH), :] = tile

    for j in range(8):
        ln = slice(128 * j, 128 * j + 128)
        for side in range(2):
            shift = -8 if side == 0 else 128
            for i, t in enumerate(RED_ROWS[side]):
                spread(r_a, PITCH, j, t + shift, hu[side, i, :, ln])
            for i, t in enumerate(BLACK_ROWS[side]):
                spread(b_a, PITCH, j, t + shift, hu[side, 5 + i, :, ln])
            for i, (t, colour) in enumerate(COEF_ROWS[side]):
                spread(sg, colour * NK * PITCH, j, t + shift, hs[side, i, :, ln].astype(F32) * SIXTY)
                spread(jg, colour * NK * PITCH, j, t + shift, hc[side, i, :, ln].astype(F32))

    for c in first_hop + second_hop + time_hop + az_hop + diag_hop: c.wait_send()

    @pl.when(az == NAZ - 1)
    def _():
        for c in beyond[0]: c.wait_send()

    @pl.when(az == 0)
    def _():
        for c in beyond[1]: c.wait_send()


def relax(r_0, b_0, sg, jg, out_hbm, r_1, b_1, r_2, outs, out_sem):
    rowi = lax.broadcasted_iota(jnp.int32, (8, 128), 0)
    lane = lax.broadcasted_iota(jnp.int32, (8, 128), 1)
    odd = ((rowi + lane) & 1) == 1
    first, last = lane == 0, lane == 127

    def out_copy(k, slot):
        return pltpu.make_async_copy(outs.at[slot], out_hbm.at[pl.ds(2 * k, 2)], out_sem.at[slot])

    zero = jnp.zeros((8, 128), F32)
    for j in range(NJ):
        for i in range(ROWS // 8):
            x = r_0[pl.ds(row(0, j, 8 * i), 8), :]
            for ref in (r_1, b_1, r_2):
                ref[pl.ds(row(NK + 1, j, 8 * i), 8), :] = zero
                ref[pl.ds(row(0, j, 8 * i), 8), :] = x

    def half(k, colour, src, own, rho, nj, emit):
        st = (k + 1) * PITCH
        co = (k + colour * NK) * PITCH
        cen = [src[pl.ds(st + j * ROWS + rho, 8), :] for j in range(NJ)]
        rl = [pltpu.roll(x, 1, 1) for x in cen]
        rr = [pltpu.roll(x, 127, 1) for x in cen]
        for j in range(nj):
            off = j * ROWS + rho
            left = jnp.where(first, rl[(j - 1) % NJ], rl[j])
            right = jnp.where(last, rr[(j + 1) % NJ], rr[j])
            lo, hi = src[pl.ds(st - PITCH + off, 8), :], src[pl.ds(st + PITCH + off, 8), :]
            rad = jnp.where(odd, hi, lo) if colour == 0 else jnp.where(odd, lo, hi)
            d1 = src[pl.ds(st + off + 1, 8), :] - src[pl.ds(st + off - 1, 8), :]
            d2 = own[pl.ds(st + off + 2, 8), :] - own[pl.ds(st + off - 2, 8), :]
            acc = ((jg[pl.ds(co + off, 8), :] + rad) + cen[j]) + (left + right)
            emit(j, rho, acc * 0.25 - sg[pl.ds(co + off, 8), :] * (d1 * 8.0 - d2))

    def unit(k, colour, src, own, dst):
        st = (k + 1) * PITCH

        def emit(j, rho, val):
            dst[pl.ds(st + j * ROWS + rho, 8), :] = val
        for i in range(17):
            half(k, colour, src, own, 8 + 8 * i, NJ, emit)

    def final(k, slot):
        st = (k + 1) * PITCH

        def emit(j, rho, val):
            red = r_2[pl.ds(st + j * ROWS + rho, 8), :]
            t = rho - T0
            outs[slot, 0, t:t + 8, 128 * j:128 * j + 128] = jnp.where(odd, val, red)
            outs[slot, 1, t:t + 8, 128 * j:128 * j + 128] = jnp.where(odd, red, val)
        for i in range(16):
            half(k, 1, r_2, b_1, T0 + 8 * i, 8, emit)

    def step(s, _):
        @pl.when(s < NK)
        def _():
            unit(NK - 1 - s, 0, b_0, r_0, r_1)

        @pl.when((s >= 1) & (s < NK + 1))
        def _():
            unit(NK - s, 1, r_1, b_0, b_1)

        @pl.when((s >= 2) & (s < NK + 2))
        def _():
            unit(NK + 1 - s, 0, b_1, r_1, r_2)

        @pl.when(s >= 3)
        def _():
            k = NK + 2 - s
            slot = lax.rem(s, 2)

            @pl.when(s >= 5)
            def _():
                out_copy(k + 2, slot).wait()
            final(k, slot)
            out_copy(k, slot).start()
        return 0
    lax.fori_loop(0, NK + 3, step, 0)
    out_copy(1, 1).wait()
    out_copy(0, 0).wait()


def local(u, s, c, rot, skew):
    sk = jnp.broadcast_to(skew[:, None], (128, 128))
    anys = pl.BlockSpec(memory_space=pl.ANY)
    vm = pl.BlockSpec(memory_space=pltpu.VMEM)
    D, V = pltpu.SemaphoreType.DMA, pltpu.VMEM
    state = V(((NK + 2) * PITCH, 128), F32)
    coef = V((2 * NK * PITCH, 128), F32)
    packed = pl.pallas_call(
        exchange,
        out_shape=(state, state, coef, coef),
        in_specs=[anys] * 4 + [vm],
        out_specs=(vm,) * 4,
        scratch_shapes=[V((2, 2, 128, 1024), F32), V((2, 2, 128, 1024), BF16), V((2, 2, 128, 1024), BF16),
                        V((2, 16, 8, 1024), F32), V((2, 16, 8, 1024), BF16), V((2, 16, 8, 1024), BF16),
                        V((3 * 2 * 8 * 128, 128), F32),
                        V((2, 9, 8, 1024), F32), V((2, 5, 8, 1024), BF16), V((2, 5, 8, 1024), BF16),
                        V((2, 9, 8, 1024), F32), V((2, 5, 8, 1024), BF16), V((2, 5, 8, 1024), BF16),
                        V((2, 16, 128, 128), F32), V((2, 16, 128, 128), BF16), V((2, 16, 128, 128), BF16),
                        V((128, 128), F32), V((128, 128), BF16), V((128, 128), BF16), V((2, 3, 8, 128), F32),
                        V((2, 128, 128), F32), V((2, 128, 128), BF16), V((2, 128, 128), BF16), V((2, 2, 3, 8, 128), F32),
                        V((16, 8192), BF16), V((16, 8192), BF16), V((8, 9, 16, 128), BF16),
                        V((9, 128, 128), BF16), V((2, 9, 16, 128), BF16),
                        D((3, 2)), D((3, 2)), D((3, 2)), D((2,)), D((7,)), D((7,)), D((7,)), D((7,)), D((2, 3)), D((2, 3)),
                        D((2, 3)), D((2, 3)), D((2, 2)), D((2, 2)), D((8,)), D((2,))],
        compiler_params=pltpu.CompilerParams(collective_id=0, has_side_effects=True, vmem_limit_bytes=LIMIT),
        name="exchange",
    )(u, s, c, rot, sk)
    return pl.pallas_call(
        relax,
        out_shape=jax.ShapeDtypeStruct((16, 128, 1024), F32),
        in_specs=[vm] * 4,
        out_specs=anys,
        scratch_shapes=[state, state, state, V((2, 2, 128, 1024), F32), D((2,))],
        compiler_params=pltpu.CompilerParams(vmem_limit_bytes=LIMIT2),
        name="relax",
    )(*[pltpu.with_memory_space_constraint(x, pltpu.VMEM) for x in packed])


def solution(mesh):
    placed = (P(None, "ta", "az"), P(None, "ta", "az"), P(None, "ta", "az"), P("ta", "az"), P("ta"))
    return jax.shard_map(
        local, mesh=mesh, in_specs=placed, out_specs=P(None, "ta", "az"), check_vma=False
    )
```

```python
import jax
import jax.numpy as jnp
from jax import lax
from jax.experimental import pallas as pl
from jax.experimental.pallas import tpu as pltpu
from jax.sharding import PartitionSpec as P

F32, BF16 = jnp.float32, jnp.bfloat16
MESH = pl.DeviceIdType.MESH
NAZ, NTA = 8, 16
NK, NJ, ROWS, T0 = 8, 9, 152, 12
PITCH = NJ * ROWS
SIXTY = 1.0 / 48.0
LIMIT = 16100 * 1024
RED_ROWS = ((3, 4, 5, 6, 7), (0, 1, 2, 3, 4))
BLACK_ROWS = ((7, 6, 5, 4), (0, 1, 2, 3))
COEF_ROWS = (((5, 0), (6, 0), (7, 0), (6, 1), (7, 1)), ((0, 0), (1, 0), (2, 0), (0, 1), (1, 1)))


def row(kk, j, rho):
    return kk * PITCH + j * ROWS + rho


def sweep(fn, top, bottom):
    def one(i, _):
        fn(top - i)
        return 0
    lax.fori_loop(0, top - bottom + 1, one, 0)


def half(k, colour, src, own, sg, jg, rho, nj, emit):
    rowi = lax.broadcasted_iota(jnp.int32, (8, 128), 0)
    lane = lax.broadcasted_iota(jnp.int32, (8, 128), 1)
    odd = ((rowi + lane) & 1) == 1
    first, last = lane == 0, lane == 127
    st = (k + 1) * PITCH
    co = (k + colour * NK) * PITCH
    cen = [src[pl.ds(st + j * ROWS + rho, 8), :] for j in range(NJ)]
    rl = [pltpu.roll(x, 1, 1) for x in cen]
    rr = [pltpu.roll(x, 127, 1) for x in cen]
    for j in range(nj):
        off = j * ROWS + rho
        left = jnp.where(first, rl[(j - 1) % NJ], rl[j])
        right = jnp.where(last, rr[(j + 1) % NJ], rr[j])
        lo, hi = src[pl.ds(st - PITCH + off, 8), :], src[pl.ds(st + PITCH + off, 8), :]
        rad = jnp.where(odd, hi, lo) if colour == 0 else jnp.where(odd, lo, hi)
        d1 = src[pl.ds(st + off + 1, 8), :] - src[pl.ds(st + off - 1, 8), :]
        d2 = own[pl.ds(st + off + 2, 8), :] - own[pl.ds(st + off - 2, 8), :]
        acc = ((jg[pl.ds(co + off, 8), :] + rad) + cen[j]) + (left + right)
        emit(j, rho, acc * 0.25 - sg[pl.ds(co + off, 8), :] * (d1 * 8.0 - d2))


def update(k, colour, src, own, dst, sg, jg, tiles):
    st = (k + 1) * PITCH

    def emit(j, rho, val):
        dst[pl.ds(st + j * ROWS + rho, 8), :] = val
    for i in tiles:
        half(k, colour, src, own, sg, jg, 8 + 8 * i, NJ, emit)


def exchange(u_hbm, s_hbm, c_hbm, rot_hbm, sk, r_a, b_a, sg, jg, r_b, b_b,
             us, ss, cs, eu, es, ec, er, su, tb, hu, hb, ku, ks, kc, pu, ps, pc, pd, fu, fs, fc, qu, qs, qc, qd,
             w0, w1, v, cyc, cych,
             in_sem, edge_sem, col_sem, own_sem, p1s, p1r, p3s, p3r, azs, azr, tas, tar, dis, dir_, cys, cyr):
    az, ta = lax.axis_index("az"), lax.axis_index("ta")
    up, down = lax.rem(ta + NTA - 1, NTA), lax.rem(ta + 1, NTA)
    left_az, right_az = lax.rem(az + NAZ - 1, NAZ), lax.rem(az + 1, NAZ)
    others = [lax.rem(az + o, NAZ) for o in range(1, NAZ)]
    diagonals = [(side, other, t, a) for side, t in ((0, down), (1, up)) for other, a in ((0, right_az), (1, left_az))]

    rowi = lax.broadcasted_iota(jnp.int32, (8, 128), 0)
    lane = lax.broadcasted_iota(jnp.int32, (8, 128), 1)
    odd = ((rowi + lane) & 1) == 1
    lane16 = lax.broadcasted_iota(jnp.int32, (16, 128), 1)
    row16 = lax.broadcasted_iota(jnp.int32, (16, 128), 0)
    odd16 = ((lane16 + row16) & 1) == 1
    low16 = lane16 < 64

    def remote(src, dst, ssem, rsem, dev):
        return pltpu.make_async_remote_copy(src_ref=src, dst_ref=dst, send_sem=ssem, recv_sem=rsem,
                                            device_id=dev, device_id_type=MESH)

    def in_copies(k, slot):
        pair = pl.ds(2 * k, 2)
        return [pltpu.make_async_copy(h.at[pair], dst.at[slot], in_sem.at[i, slot])
                for i, (h, dst) in enumerate(((u_hbm, us), (s_hbm, ss), (c_hbm, cs)))]

    edges = [pltpu.make_async_copy(h.at[:, pl.ds(t, 8), :], e.at[side], edge_sem.at[q, side])
             for q, (h, e) in enumerate(((u_hbm, eu), (s_hbm, es), (c_hbm, ec))) for side, t in ((0, 120), (1, 0))]
    cols = [pltpu.make_async_copy(h.at[:, :, pl.ds(n, 128)], e.at[side], col_sem.at[q, side])
            for q, (h, e) in enumerate(((u_hbm, ku), (s_hbm, ks), (c_hbm, kc))) for side, n in ((0, 0), (1, 896))]

    barrier = pltpu.get_barrier_semaphore()
    for d in others:
        pl.semaphore_signal(barrier, inc=1, device_id={"az": d}, device_id_type=MESH)
    for t in (up, down):
        for a in range(NAZ):
            pl.semaphore_signal(barrier, inc=1, device_id={"ta": t, "az": a}, device_id_type=MESH)
    for c in edges: c.start()
    for c in cols: c.start()
    own = pltpu.make_async_copy(rot_hbm.at[pl.ds(16 * az, 16), :], w0.at[:, pl.ds(1024 * az, 1024)], own_sem.at[0])
    own.start()
    for c in in_copies(NK - 1, 0): c.start()
    for c in in_copies(NK - 2, 1): c.start()
    pl.semaphore_wait(barrier, 3 * NAZ - 1)
    first_hop = [remote(rot_hbm.at[pl.ds(16 * d, 16), :], w0.at[:, pl.ds(1024 * az, 1024)], p1s.at[o], p1r.at[o], {"az": d})
                 for o, d in enumerate(others)]
    for c in first_hop: c.start()

    for c in edges: c.wait()
    for side in range(2):
        for q, e in enumerate((eu, es, ec)):
            for j in range(8):
                ln = slice(128 * j, 128 * j + 128)
                base = (side * 8 + j) * 128
                for k in range(NK):
                    even, odd_layer = e[side, 2 * k, :, ln].astype(F32), e[side, 2 * k + 1, :, ln].astype(F32)
                    er[base + 8 * k:base + 8 * k + 8, :] = jnp.where(odd, odd_layer, even)
                    er[base + 64 + 8 * k:base + 72 + 8 * k, :] = jnp.where(odd, even, odd_layer)
                if q == 0:
                    for i, t in enumerate(RED_ROWS[side]):
                        tb[side, i, :, ln] = er[pl.ds(base + t, NK, stride=8), :].astype(BF16)
                    for i, t in enumerate(BLACK_ROWS[side]):
                        tile = er[pl.ds(base + 64 + t, NK, stride=8), :]
                        if i < 2:
                            su[side, i, :, ln] = tile
                        else:
                            tb[side, 3 + i, :, ln] = tile.astype(BF16)
                else:
                    for i, (t, colour) in enumerate(COEF_ROWS[side]):
                        tb[side, 2 + 5 * q + i, :, ln] = er[pl.ds(base + 64 * colour + t, NK, stride=8), :].astype(BF16)
    time_hop = [remote(a.at[side], b.at[side], tas.at[side, q], tar.at[side, q], {"ta": d})
                for side, d in ((0, down), (1, up)) for q, (a, b) in enumerate(((su, hu), (tb, hb)))]
    for c in time_hop: c.start()

    for c in cols: c.wait()

    def columns(i, _):
        rows = pl.ds(pl.multiple_of(16 * i, 16), 16)
        for src, dst in ((ku, pu), (ks, ps), (kc, pc)):
            acc = jnp.zeros((16, 128), F32)
            for k in range(NK):
                even = jnp.where(low16, src[0, 2 * k, rows, :].astype(F32), src[1, 2 * k, rows, :].astype(F32))
                odd_l = jnp.where(low16, src[0, 2 * k + 1, rows, :].astype(F32), src[1, 2 * k + 1, rows, :].astype(F32))
                red, black = jnp.where(odd16, odd_l, even), jnp.where(odd16, even, odd_l)
                for a, x in ((k, red), (k + 8, black)):
                    acc = jnp.where((lane16 >> 3) == a, pltpu.roll(x, (8 * a + 4) % 128, 1), acc)
            dst[rows, :] = acc.astype(dst.dtype)
        return 0
    lax.fori_loop(0, 8, columns, 0)
    for q, src in enumerate((pu, ps, pc)):
        pd[0, q] = src[112:128, :].astype(F32)[8:]
        pd[1, q] = src[0:16, :].astype(F32)[:8]
    mine16 = (lane16 & 7) < 4
    for src, dst in ((pu, fu), (ps, fs), (pc, fc)):
        for i in range(4):
            early, late = src[16 * i:16 * i + 16, :].astype(F32), src[64 + 16 * i:80 + 16 * i, :].astype(F32)
            dst[0, 16 * i:16 * i + 16, :] = jnp.where(mine16, early, pltpu.roll(late, 4, 1)).astype(dst.dtype)
            dst[1, 16 * i:16 * i + 16, :] = jnp.where(mine16, pltpu.roll(early, 124, 1), late).astype(dst.dtype)
    az_hop = [remote(a.at[side], b.at[side], azs.at[side, q], azr.at[side, q], {"az": d})
              for side, d in ((0, right_az), (1, left_az)) for q, (a, b) in enumerate(((fu, qu), (fs, qs), (fc, qc)))]
    diag_hop = [remote(pd.at[side], qd.at[side, other], dis.at[side, other], dir_.at[side, other], {"ta": t, "az": a})
                for side, other, t, a in diagonals]
    for c in az_hop + diag_hop: c.start()

    def pack(s, _):
        k = NK - 1 - s
        slot = lax.rem(s, 2)
        for c in in_copies(k, slot): c.wait()
        st, c0, c1 = (k + 1) * PITCH, k * PITCH, (k + NK) * PITCH
        for i in range(8):
            rows = slice(16 * i, 16 * i + 16)
            for j in range(8):
                ln = slice(128 * j, 128 * j + 128)
                e16, o16 = ss[slot, 0, rows, ln].astype(F32) * SIXTY, ss[slot, 1, rows, ln].astype(F32) * SIXTY
                f16, p16 = cs[slot, 0, rows, ln].astype(F32), cs[slot, 1, rows, ln].astype(F32)
                for h in range(2):
                    part, r8 = slice(8 * h, 8 * h + 8), slice(16 * i + 8 * h, 16 * i + 8 * h + 8)
                    at = j * ROWS + T0 + 16 * i + 8 * h
                    for e, o, ra, rb, pa, pb in ((us[slot, 0, r8, ln], us[slot, 1, r8, ln], r_a, b_a, st, st),
                                                 (e16[part], o16[part], sg, sg, c0, c1), (f16[part], p16[part], jg, jg, c0, c1)):
                        ra[pl.ds(pa + at, 8), :] = jnp.where(odd, o, e)
                        rb[pl.ds(pb + at, 8), :] = jnp.where(odd, e, o)

        @pl.when(s + 2 < NK)
        def _():
            for c in in_copies(k - 2, slot): c.start()
        return 0

    own.wait()
    for c in first_hop: c.wait_recv()
    amount = sk[pl.ds(pl.multiple_of(16 * az, 16), 16), :]
    src, dst = w0, w1
    for b in range(6):
        bit = ((amount >> b) & 1) == 1
        for p in range(64):
            f = (p - (1 << b)) % 64
            dst[:, 128 * p:128 * p + 128] = jnp.where(bit, src[:, 128 * f:128 * f + 128], src[:, 128 * p:128 * p + 128])
        src, dst = dst, src
    for d in range(NAZ):
        for jj in range(8):
            v[d, jj] = w0[:, 1024 * d + 128 * jj:1024 * d + 128 * jj + 128]
        after, before = (8 * d + 8) % 64, (8 * d - 1) % 64
        v[d, 8] = jnp.where(low16, w0[:, 128 * after:128 * after + 128], w0[:, 128 * before:128 * before + 128])
    block = pl.ds(16 * az, 16)
    mine = pltpu.make_async_copy(v.at[az], cyc.at[:, block, :], own_sem.at[1])
    mine.start()
    second_hop = [remote(v.at[d], cyc.at[:, block, :], p3s.at[o], p3r.at[o], {"az": d}) for o, d in enumerate(others)]
    for c in second_hop: c.start()
    beyond = [[remote(v.at[d], cych.at[side], cys.at[d], cyr.at[side], {"ta": t, "az": d}) for d in range(NAZ)]
              for side, t in ((0, down), (1, up))]

    @pl.when(az == NAZ - 1)
    def _():
        for c in beyond[0]: c.start()

    @pl.when(az == 0)
    def _():
        for c in beyond[1]: c.start()

    lax.fori_loop(0, NK, pack, 0)

    zero = jnp.zeros((8, 128), F32)
    for j in range(NJ):
        for i in range(ROWS // 8):
            for ref in (b_a, r_b, b_b):
                ref[pl.ds(row(NK + 1, j, 8 * i), 8), :] = zero

    for c in az_hop: c.wait_recv()
    for c in diag_hop: c.wait_recv()
    mine_lane = (lane & 7) < 4

    def place(q, x, rho):
        if q == 1:
            x = x * SIXTY
        for a in range(16):
            y = pltpu.roll(x, (124 - 8 * a) % 128, 1)
            if q == 0:
                (r_a if a < 8 else b_a)[pl.ds(row(a % 8 + 1, NJ - 1, rho), 8), :] = y
            else:
                (sg if q == 1 else jg)[pl.ds(a * PITCH + (NJ - 1) * ROWS + rho, 8), :] = y

    for q, b in enumerate((qu, qs, qc)):
        for side, rho in ((0, T0 - 8), (1, T0 + 128)):
            place(q, jnp.where(mine_lane, qd[side, 0, q], qd[side, 1, q]), rho)
        for i in range(4):
            lt, rt = b[0, 16 * i:16 * i + 16, :].astype(F32), b[1, 16 * i:16 * i + 16, :].astype(F32)
            early = jnp.where(mine16, lt, pltpu.roll(rt, 4, 1))
            late = jnp.where(mine16, pltpu.roll(lt, 124, 1), rt)
            for h in range(2):
                place(q, early[8 * h:8 * h + 8], T0 + 16 * i + 8 * h)
                place(q, late[8 * h:8 * h + 8], T0 + 64 + 16 * i + 8 * h)

    sweep(lambda k: update(k, 0, b_a, r_a, r_b, sg, jg, range(1, 16)), 7, 1)
    sweep(lambda k: update(k, 1, r_b, b_a, b_b, sg, jg, range(2, 15)), 7, 2)

    mine.wait()
    for c in second_hop: c.wait_recv()
    for side in range(2): beyond[side][0].wait_recv()
    for j in range(NJ):
        for i in range(8):
            x = cyc[j, 16 * i:16 * i + 16, :].astype(F32)
            for ref in (b_a, r_b, b_b):
                ref[pl.ds(row(0, j, T0 + 16 * i), 16), :] = x
        top, bottom = cych[0, j].astype(F32)[8:], cych[1, j].astype(F32)[:8]
        for ref in (b_a, r_b, b_b):
            ref[pl.ds(row(0, j, T0 - 8), 8), :] = top
            ref[pl.ds(row(0, j, T0 + 128), 8), :] = bottom

    for c in time_hop: c.wait_recv()

    def spread(ref, base, j, t, tile):
        ref[pl.ds(base + j * ROWS + T0 + t, NK, stride=PITCH), :] = tile

    for j in range(8):
        ln = slice(128 * j, 128 * j + 128)
        for side in range(2):
            shift = -8 if side == 0 else 128
            for i, t in enumerate(RED_ROWS[side]):
                spread(r_a, PITCH, j, t + shift, hb[side, i, :, ln].astype(F32))
            for i, t in enumerate(BLACK_ROWS[side]):
                spread(b_a, PITCH, j, t + shift, hu[side, i, :, ln] if i < 2 else hb[side, 3 + i, :, ln].astype(F32))
            for i, (t, colour) in enumerate(COEF_ROWS[side]):
                spread(sg, colour * NK * PITCH, j, t + shift, hb[side, 7 + i, :, ln].astype(F32) * SIXTY)
                spread(jg, colour * NK * PITCH, j, t + shift, hb[side, 12 + i, :, ln].astype(F32))

    for c in first_hop + second_hop + time_hop + az_hop + diag_hop: c.wait_send()

    @pl.when(az == NAZ - 1)
    def _():
        for c in beyond[0]: c.wait_send()

    @pl.when(az == 0)
    def _():
        for c in beyond[1]: c.wait_send()


def relax(r_0, b_0, sg, jg, _r, _b, out_hbm, r_1, b_1, r_2, outs, out_sem):
    rowi = lax.broadcasted_iota(jnp.int32, (8, 128), 0)
    lane = lax.broadcasted_iota(jnp.int32, (8, 128), 1)
    odd = ((rowi + lane) & 1) == 1

    def out_copy(k, slot):
        return pltpu.make_async_copy(outs.at[slot], out_hbm.at[pl.ds(2 * k, 2)], out_sem.at[slot])

    zero = jnp.zeros((8, 128), F32)
    for j in range(NJ):
        for i in range(ROWS // 8):
            r_2[pl.ds(row(NK + 1, j, 8 * i), 8), :] = zero
            r_2[pl.ds(row(0, j, 8 * i), 8), :] = b_0[pl.ds(row(0, j, 8 * i), 8), :]

    def final(k, slot):
        st = (k + 1) * PITCH

        def emit(j, rho, val):
            red = r_2[pl.ds(st + j * ROWS + rho, 8), :]
            t = rho - T0
            outs[slot, 0, t:t + 8, 128 * j:128 * j + 128] = jnp.where(odd, val, red)
            outs[slot, 1, t:t + 8, 128 * j:128 * j + 128] = jnp.where(odd, red, val)
        for i in range(16):
            half(k, 1, r_2, b_1, sg, jg, T0 + 8 * i, 8, emit)

    edge_0, edge_1 = (0, 16), (0, 1, 15, 16)

    def step(s, _):
        @pl.when(s < NK - 1)
        def _():
            update(NK - 1 - s, 0, b_0, r_0, r_1, sg, jg, edge_0)

        @pl.when(s == NK - 1)
        def _():
            update(0, 0, b_0, r_0, r_1, sg, jg, range(17))

        @pl.when((s >= 1) & (s < NK - 1))
        def _():
            update(NK - s, 1, r_1, b_0, b_1, sg, jg, edge_1)

        @pl.when((s >= NK - 1) & (s < NK + 1))
        def _():
            update(NK - s, 1, r_1, b_0, b_1, sg, jg, range(17))

        @pl.when((s >= 2) & (s < NK + 2))
        def _():
            update(NK + 1 - s, 0, b_1, r_1, r_2, sg, jg, range(17))

        @pl.when(s >= 3)
        def _():
            k = NK + 2 - s
            slot = lax.rem(s, 2)

            @pl.when(s >= 5)
            def _():
                out_copy(k + 2, slot).wait()
            final(k, slot)
            out_copy(k, slot).start()
        return 0
    lax.fori_loop(0, NK + 3, step, 0)
    out_copy(1, 1).wait()
    out_copy(0, 0).wait()


def local(u, s, c, rot, skew):
    sk = jnp.broadcast_to(skew[:, None], (128, 128))
    anys = pl.BlockSpec(memory_space=pl.ANY)
    vm = pl.BlockSpec(memory_space=pltpu.VMEM)
    D, V = pltpu.SemaphoreType.DMA, pltpu.VMEM
    state = V(((NK + 2) * PITCH, 128), F32)
    coef = V((2 * NK * PITCH, 128), F32)
    packed = pl.pallas_call(
        exchange,
        out_shape=(state, state, coef, coef, state, state),
        in_specs=[anys] * 4 + [vm],
        out_specs=(vm,) * 6,
        scratch_shapes=[V((2, 2, 128, 1024), F32), V((2, 2, 128, 1024), BF16), V((2, 2, 128, 1024), BF16),
                        V((2, 16, 8, 1024), F32), V((2, 16, 8, 1024), BF16), V((2, 16, 8, 1024), BF16),
                        V((2 * 8 * 128, 128), F32),
                        V((2, 2, 8, 1024), F32), V((2, 17, 8, 1024), BF16),
                        V((2, 2, 8, 1024), F32), V((2, 17, 8, 1024), BF16),
                        V((2, 16, 128, 128), F32), V((2, 16, 128, 128), BF16), V((2, 16, 128, 128), BF16),
                        V((128, 128), F32), V((128, 128), BF16), V((128, 128), BF16), V((2, 3, 8, 128), F32),
                        V((2, 64, 128), F32), V((2, 64, 128), BF16), V((2, 64, 128), BF16),
                        V((2, 64, 128), F32), V((2, 64, 128), BF16), V((2, 64, 128), BF16), V((2, 2, 3, 8, 128), F32),
                        V((16, 8192), BF16), V((16, 8192), BF16), V((8, 9, 16, 128), BF16),
                        V((9, 128, 128), BF16), V((2, 9, 16, 128), BF16),
                        D((3, 2)), D((3, 2)), D((3, 2)), D((2,)), D((7,)), D((7,)), D((7,)), D((7,)), D((2, 3)), D((2, 3)),
                        D((2, 2)), D((2, 2)), D((2, 2)), D((2, 2)), D((8,)), D((2,))],
        compiler_params=pltpu.CompilerParams(collective_id=0, has_side_effects=True, vmem_limit_bytes=LIMIT),
        name="exchange",
    )(u, s, c, rot, sk)
    out, _, _ = pl.pallas_call(
        relax,
        out_shape=(jax.ShapeDtypeStruct((16, 128, 1024), F32), state, state),
        in_specs=[vm] * 6,
        out_specs=(anys, vm, vm),
        scratch_shapes=[state, V((2, 2, 128, 1024), F32), D((2,))],
        input_output_aliases={4: 1, 5: 2},
        compiler_params=pltpu.CompilerParams(vmem_limit_bytes=LIMIT),
        name="relax",
    )(*[pltpu.with_memory_space_constraint(x, pltpu.VMEM) for x in packed])
    return out


def solution(mesh):
    placed = (P(None, "ta", "az"), P(None, "ta", "az"), P(None, "ta", "az"), P("ta", "az"), P("ta"))
    return jax.shard_map(
        local, mesh=mesh, in_specs=placed, out_specs=P(None, "ta", "az"), check_vma=False
    )
```

```python
import jax
import jax.numpy as jnp
from jax import lax
from jax.experimental import pallas as pl
from jax.experimental.pallas import tpu as pltpu
from jax.sharding import PartitionSpec as P

F32, BF16 = jnp.float32, jnp.bfloat16
MESH = pl.DeviceIdType.MESH
NAZ, NTA = 8, 16
NK, NJ, ROWS, T0 = 8, 9, 152, 12
PITCH = NJ * ROWS
SIXTY = 1.0 / 48.0
LIMIT = 16100 * 1024
RED_ROWS = ((3, 4, 5, 6, 7), (0, 1, 2, 3, 4))
BLACK_ROWS = ((7, 6, 5, 4), (0, 1, 2, 3))
COEF_ROWS = (((5, 0), (6, 0), (7, 0), (6, 1), (7, 1)), ((0, 0), (1, 0), (2, 0), (0, 1), (1, 1)))


def row(kk, j, rho):
    return kk * PITCH + j * ROWS + rho


def sweep(fn, top, bottom):
    def one(i, _):
        fn(top - i)
        return 0
    lax.fori_loop(0, top - bottom + 1, one, 0)


def half(k, colour, src, own, sg, jg, rho, nj, emit):
    rowi = lax.broadcasted_iota(jnp.int32, (8, 128), 0)
    lane = lax.broadcasted_iota(jnp.int32, (8, 128), 1)
    odd = ((rowi + lane) & 1) == 1
    first, last = lane == 0, lane == 127
    st = (k + 1) * PITCH
    co = (k + colour * NK) * PITCH
    cen = [src[pl.ds(st + j * ROWS + rho, 8), :] for j in range(NJ)]
    rl = [pltpu.roll(x, 1, 1) for x in cen]
    rr = [pltpu.roll(x, 127, 1) for x in cen]
    for j in range(nj):
        off = j * ROWS + rho
        left = jnp.where(first, rl[(j - 1) % NJ], rl[j])
        right = jnp.where(last, rr[(j + 1) % NJ], rr[j])
        lo, hi = src[pl.ds(st - PITCH + off, 8), :], src[pl.ds(st + PITCH + off, 8), :]
        rad = jnp.where(odd, hi, lo) if colour == 0 else jnp.where(odd, lo, hi)
        d1 = src[pl.ds(st + off + 1, 8), :] - src[pl.ds(st + off - 1, 8), :]
        d2 = own[pl.ds(st + off + 2, 8), :] - own[pl.ds(st + off - 2, 8), :]
        acc = ((jg[pl.ds(co + off, 8), :] + rad) + cen[j]) + (left + right)
        emit(j, rho, acc * 0.25 - sg[pl.ds(co + off, 8), :] * (d1 * 8.0 - d2))


def update(k, colour, src, own, dst, sg, jg, tiles):
    st = (k + 1) * PITCH

    def emit(j, rho, val):
        dst[pl.ds(st + j * ROWS + rho, 8), :] = val
    for i in tiles:
        half(k, colour, src, own, sg, jg, 8 + 8 * i, NJ, emit)


def exchange(u_hbm, s_hbm, c_hbm, rot_hbm, sk, r_a, b_a, sg, jg, r_b, b_b,
             us, ss, cs, eu, es, ec, er, su, tb, hu, hb, ku, ks, kc, pu, ps, pc, pd, fu, fs, fc, qu, qs, qc, qd,
             w0, w1, v, cyc, cych,
             in_sem, edge_sem, col_sem, own_sem, p1s, p1r, p3s, p3r, azs, azr, tas, tar, dis, dir_, cys, cyr):
    az, ta = lax.axis_index("az"), lax.axis_index("ta")
    up, down = lax.rem(ta + NTA - 1, NTA), lax.rem(ta + 1, NTA)
    left_az, right_az = lax.rem(az + NAZ - 1, NAZ), lax.rem(az + 1, NAZ)
    others = [lax.rem(az + o, NAZ) for o in range(1, NAZ)]
    diagonals = [(side, other, t, a) for side, t in ((0, down), (1, up)) for other, a in ((0, right_az), (1, left_az))]

    rowi = lax.broadcasted_iota(jnp.int32, (8, 128), 0)
    lane = lax.broadcasted_iota(jnp.int32, (8, 128), 1)
    odd = ((rowi + lane) & 1) == 1
    lane16 = lax.broadcasted_iota(jnp.int32, (16, 128), 1)
    row16 = lax.broadcasted_iota(jnp.int32, (16, 128), 0)
    odd16 = ((lane16 + row16) & 1) == 1
    low16 = lane16 < 64

    def remote(src, dst, ssem, rsem, dev):
        return pltpu.make_async_remote_copy(src_ref=src, dst_ref=dst, send_sem=ssem, recv_sem=rsem,
                                            device_id=dev, device_id_type=MESH)

    def in_copies(k, slot):
        pair = pl.ds(2 * k, 2)
        return [pltpu.make_async_copy(h.at[pair], dst.at[slot], in_sem.at[i, slot])
                for i, (h, dst) in enumerate(((u_hbm, us), (s_hbm, ss), (c_hbm, cs)))]

    edges = [pltpu.make_async_copy(h.at[:, pl.ds(t, 8), :], e.at[side], edge_sem.at[q, side])
             for q, (h, e) in enumerate(((u_hbm, eu), (s_hbm, es), (c_hbm, ec))) for side, t in ((0, 120), (1, 0))]
    cols = [pltpu.make_async_copy(h.at[:, :, pl.ds(n, 128)], e.at[side], col_sem.at[q, side])
            for q, (h, e) in enumerate(((u_hbm, ku), (s_hbm, ks), (c_hbm, kc))) for side, n in ((0, 0), (1, 896))]

    barrier = pltpu.get_barrier_semaphore()
    for d in others:
        pl.semaphore_signal(barrier, inc=1, device_id={"az": d}, device_id_type=MESH)
    for t in (up, down):
        for a in range(NAZ):
            pl.semaphore_signal(barrier, inc=1, device_id={"ta": t, "az": a}, device_id_type=MESH)
    for c in cols: c.start()
    for c in edges: c.start()
    own = pltpu.make_async_copy(rot_hbm.at[pl.ds(16 * az, 16), :], w0.at[:, pl.ds(1024 * az, 1024)], own_sem.at[0])
    own.start()
    for c in in_copies(NK - 1, 0): c.start()
    for c in in_copies(NK - 2, 1): c.start()
    pl.semaphore_wait(barrier, 3 * NAZ - 1)
    first_hop = [remote(rot_hbm.at[pl.ds(16 * d, 16), :], w0.at[:, pl.ds(1024 * az, 1024)], p1s.at[o], p1r.at[o], {"az": d})
                 for o, d in enumerate(others)]
    for c in first_hop: c.start()

    for c in cols: c.wait()

    def columns(i, _):
        rows = pl.ds(pl.multiple_of(16 * i, 16), 16)
        for src, dst in ((ku, pu), (ks, ps), (kc, pc)):
            acc = jnp.zeros((16, 128), F32)
            for k in range(NK):
                even = jnp.where(low16, src[0, 2 * k, rows, :].astype(F32), src[1, 2 * k, rows, :].astype(F32))
                odd_l = jnp.where(low16, src[0, 2 * k + 1, rows, :].astype(F32), src[1, 2 * k + 1, rows, :].astype(F32))
                red, black = jnp.where(odd16, odd_l, even), jnp.where(odd16, even, odd_l)
                for a, x in ((k, red), (k + 8, black)):
                    acc = jnp.where((lane16 >> 3) == a, pltpu.roll(x, (8 * a + 4) % 128, 1), acc)
            dst[rows, :] = acc.astype(dst.dtype)
        return 0
    lax.fori_loop(0, 8, columns, 0)
    for q, src in enumerate((pu, ps, pc)):
        pd[0, q] = src[112:128, :].astype(F32)[8:]
        pd[1, q] = src[0:16, :].astype(F32)[:8]
    mine16 = (lane16 & 7) < 4
    for src, dst in ((pu, fu), (ps, fs), (pc, fc)):
        for i in range(4):
            early, late = src[16 * i:16 * i + 16, :].astype(F32), src[64 + 16 * i:80 + 16 * i, :].astype(F32)
            dst[0, 16 * i:16 * i + 16, :] = jnp.where(mine16, early, pltpu.roll(late, 4, 1)).astype(dst.dtype)
            dst[1, 16 * i:16 * i + 16, :] = jnp.where(mine16, pltpu.roll(early, 124, 1), late).astype(dst.dtype)
    az_hop = [remote(a.at[side], b.at[side], azs.at[side, q], azr.at[side, q], {"az": d})
              for side, d in ((0, right_az), (1, left_az)) for q, (a, b) in enumerate(((fu, qu), (fs, qs), (fc, qc)))]
    diag_hop = [remote(pd.at[side], qd.at[side, other], dis.at[side, other], dir_.at[side, other], {"ta": t, "az": a})
                for side, other, t, a in diagonals]
    for c in az_hop + diag_hop: c.start()

    for c in edges: c.wait()
    for side in range(2):
        for q, e in enumerate((eu, es, ec)):
            for j in range(8):
                ln = slice(128 * j, 128 * j + 128)
                base = (side * 8 + j) * 128
                for k in range(NK):
                    even, odd_layer = e[side, 2 * k, :, ln].astype(F32), e[side, 2 * k + 1, :, ln].astype(F32)
                    er[base + 8 * k:base + 8 * k + 8, :] = jnp.where(odd, odd_layer, even)
                    er[base + 64 + 8 * k:base + 72 + 8 * k, :] = jnp.where(odd, even, odd_layer)
                if q == 0:
                    for i, t in enumerate(RED_ROWS[side]):
                        tb[side, i, :, ln] = er[pl.ds(base + t, NK, stride=8), :].astype(BF16)
                    for i, t in enumerate(BLACK_ROWS[side]):
                        tile = er[pl.ds(base + 64 + t, NK, stride=8), :]
                        if i < 2:
                            su[side, i, :, ln] = tile
                        else:
                            tb[side, 3 + i, :, ln] = tile.astype(BF16)
                else:
                    for i, (t, colour) in enumerate(COEF_ROWS[side]):
                        tb[side, 2 + 5 * q + i, :, ln] = er[pl.ds(base + 64 * colour + t, NK, stride=8), :].astype(BF16)
    time_hop = [remote(a.at[side], b.at[side], tas.at[side, q], tar.at[side, q], {"ta": d})
                for side, d in ((0, down), (1, up)) for q, (a, b) in enumerate(((su, hu), (tb, hb)))]
    for c in time_hop: c.start()

    def pack(s, _):
        k = NK - 1 - s
        slot = lax.rem(s, 2)
        for c in in_copies(k, slot): c.wait()
        st, c0, c1 = (k + 1) * PITCH, k * PITCH, (k + NK) * PITCH
        for i in range(8):
            rows = slice(16 * i, 16 * i + 16)
            for j in range(8):
                ln = slice(128 * j, 128 * j + 128)
                e16, o16 = ss[slot, 0, rows, ln].astype(F32) * SIXTY, ss[slot, 1, rows, ln].astype(F32) * SIXTY
                f16, p16 = cs[slot, 0, rows, ln].astype(F32), cs[slot, 1, rows, ln].astype(F32)
                for h in range(2):
                    part, r8 = slice(8 * h, 8 * h + 8), slice(16 * i + 8 * h, 16 * i + 8 * h + 8)
                    at = j * ROWS + T0 + 16 * i + 8 * h
                    for e, o, ra, rb, pa, pb in ((us[slot, 0, r8, ln], us[slot, 1, r8, ln], r_a, b_a, st, st),
                                                 (e16[part], o16[part], sg, sg, c0, c1), (f16[part], p16[part], jg, jg, c0, c1)):
                        ra[pl.ds(pa + at, 8), :] = jnp.where(odd, o, e)
                        rb[pl.ds(pb + at, 8), :] = jnp.where(odd, e, o)

        @pl.when(s + 2 < NK)
        def _():
            for c in in_copies(k - 2, slot): c.start()
        return 0

    own.wait()
    for c in first_hop: c.wait_recv()
    here = jnp.where(lane16 == row16 + 16 * az, jnp.broadcast_to(sk[...], (16, 128)).astype(F32), 0.0)
    amount = jnp.broadcast_to(jnp.sum(here, axis=1, keepdims=True).astype(jnp.int32), (16, 128))
    src, dst = w0, w1
    for b in range(6):
        bit = ((amount >> b) & 1) == 1
        for p in range(64):
            f = (p - (1 << b)) % 64
            dst[:, 128 * p:128 * p + 128] = jnp.where(bit, src[:, 128 * f:128 * f + 128], src[:, 128 * p:128 * p + 128])
        src, dst = dst, src
    for d in range(NAZ):
        for jj in range(8):
            v[d, jj] = w0[:, 1024 * d + 128 * jj:1024 * d + 128 * jj + 128]
        after, before = (8 * d + 8) % 64, (8 * d - 1) % 64
        v[d, 8] = jnp.where(low16, w0[:, 128 * after:128 * after + 128], w0[:, 128 * before:128 * before + 128])
    block = pl.ds(16 * az, 16)
    mine = pltpu.make_async_copy(v.at[az], cyc.at[:, block, :], own_sem.at[1])
    mine.start()
    second_hop = [remote(v.at[d], cyc.at[:, block, :], p3s.at[o], p3r.at[o], {"az": d}) for o, d in enumerate(others)]
    for c in second_hop: c.start()
    beyond = [[remote(v.at[d], cych.at[side], cys.at[d], cyr.at[side], {"ta": t, "az": d}) for d in range(NAZ)]
              for side, t in ((0, down), (1, up))]

    @pl.when(az == NAZ - 1)
    def _():
        for c in beyond[0]: c.start()

    @pl.when(az == 0)
    def _():
        for c in beyond[1]: c.start()

    lax.fori_loop(0, NK, pack, 0)

    zero = jnp.zeros((8, 128), F32)
    for j in range(NJ):
        for i in range(ROWS // 8):
            for ref in (b_a, r_b, b_b):
                ref[pl.ds(row(NK + 1, j, 8 * i), 8), :] = zero

    for c in az_hop: c.wait_recv()
    for c in diag_hop: c.wait_recv()
    mine_lane = (lane & 7) < 4

    def place(q, x, rho):
        if q == 1:
            x = x * SIXTY
        for a in range(16):
            y = pltpu.roll(x, (124 - 8 * a) % 128, 1)
            if q == 0:
                (r_a if a < 8 else b_a)[pl.ds(row(a % 8 + 1, NJ - 1, rho), 8), :] = y
            else:
                (sg if q == 1 else jg)[pl.ds(a * PITCH + (NJ - 1) * ROWS + rho, 8), :] = y

    for q, b in enumerate((qu, qs, qc)):
        for side, rho in ((0, T0 - 8), (1, T0 + 128)):
            place(q, jnp.where(mine_lane, qd[side, 0, q], qd[side, 1, q]), rho)
        for i in range(4):
            lt, rt = b[0, 16 * i:16 * i + 16, :].astype(F32), b[1, 16 * i:16 * i + 16, :].astype(F32)
            early = jnp.where(mine16, lt, pltpu.roll(rt, 4, 1))
            late = jnp.where(mine16, pltpu.roll(lt, 124, 1), rt)
            for h in range(2):
                place(q, early[8 * h:8 * h + 8], T0 + 16 * i + 8 * h)
                place(q, late[8 * h:8 * h + 8], T0 + 64 + 16 * i + 8 * h)

    sweep(lambda k: update(k, 0, b_a, r_a, r_b, sg, jg, range(1, 16)), 7, 1)
    sweep(lambda k: update(k, 1, r_b, b_a, b_b, sg, jg, range(2, 15)), 7, 2)

    mine.wait()
    for c in second_hop: c.wait_recv()
    for side in range(2): beyond[side][0].wait_recv()
    for j in range(NJ):
        for i in range(8):
            x = cyc[j, 16 * i:16 * i + 16, :].astype(F32)
            for ref in (b_a, r_b, b_b):
                ref[pl.ds(row(0, j, T0 + 16 * i), 16), :] = x
        top, bottom = cych[0, j].astype(F32)[8:], cych[1, j].astype(F32)[:8]
        for ref in (b_a, r_b, b_b):
            ref[pl.ds(row(0, j, T0 - 8), 8), :] = top
            ref[pl.ds(row(0, j, T0 + 128), 8), :] = bottom

    for c in time_hop: c.wait_recv()

    def spread(ref, base, j, t, tile):
        ref[pl.ds(base + j * ROWS + T0 + t, NK, stride=PITCH), :] = tile

    for j in range(8):
        ln = slice(128 * j, 128 * j + 128)
        for side in range(2):
            shift = -8 if side == 0 else 128
            for i, t in enumerate(RED_ROWS[side]):
                spread(r_a, PITCH, j, t + shift, hb[side, i, :, ln].astype(F32))
            for i, t in enumerate(BLACK_ROWS[side]):
                spread(b_a, PITCH, j, t + shift, hu[side, i, :, ln] if i < 2 else hb[side, 3 + i, :, ln].astype(F32))
            for i, (t, colour) in enumerate(COEF_ROWS[side]):
                spread(sg, colour * NK * PITCH, j, t + shift, hb[side, 7 + i, :, ln].astype(F32) * SIXTY)
                spread(jg, colour * NK * PITCH, j, t + shift, hb[side, 12 + i, :, ln].astype(F32))

    for c in first_hop + second_hop + time_hop + az_hop + diag_hop: c.wait_send()

    @pl.when(az == NAZ - 1)
    def _():
        for c in beyond[0]: c.wait_send()

    @pl.when(az == 0)
    def _():
        for c in beyond[1]: c.wait_send()


def relax(r_0, b_0, sg, jg, _r, _b, out_hbm, r_1, b_1, r_2, outs, out_sem):
    rowi = lax.broadcasted_iota(jnp.int32, (8, 128), 0)
    lane = lax.broadcasted_iota(jnp.int32, (8, 128), 1)
    odd = ((rowi + lane) & 1) == 1

    def out_copy(k, slot):
        return pltpu.make_async_copy(outs.at[slot], out_hbm.at[pl.ds(2 * k, 2)], out_sem.at[slot])

    zero = jnp.zeros((8, 128), F32)
    for j in range(NJ):
        for i in range(ROWS // 8):
            r_2[pl.ds(row(NK + 1, j, 8 * i), 8), :] = zero
            r_2[pl.ds(row(0, j, 8 * i), 8), :] = b_0[pl.ds(row(0, j, 8 * i), 8), :]

    def final(k, slot):
        st = (k + 1) * PITCH

        def emit(j, rho, val):
            red = r_2[pl.ds(st + j * ROWS + rho, 8), :]
            t = rho - T0
            outs[slot, 0, t:t + 8, 128 * j:128 * j + 128] = jnp.where(odd, val, red)
            outs[slot, 1, t:t + 8, 128 * j:128 * j + 128] = jnp.where(odd, red, val)
        for i in range(16):
            half(k, 1, r_2, b_1, sg, jg, T0 + 8 * i, 8, emit)

    edge_0, edge_1 = (0, 16), (0, 1, 15, 16)

    def step(s, _):
        @pl.when(s < NK - 1)
        def _():
            update(NK - 1 - s, 0, b_0, r_0, r_1, sg, jg, edge_0)

        @pl.when(s == NK - 1)
        def _():
            update(0, 0, b_0, r_0, r_1, sg, jg, range(17))

        @pl.when((s >= 1) & (s < NK - 1))
        def _():
            update(NK - s, 1, r_1, b_0, b_1, sg, jg, edge_1)

        @pl.when((s >= NK - 1) & (s < NK + 1))
        def _():
            update(NK - s, 1, r_1, b_0, b_1, sg, jg, range(17))

        @pl.when((s >= 2) & (s < NK + 2))
        def _():
            update(NK + 1 - s, 0, b_1, r_1, r_2, sg, jg, range(17))

        @pl.when(s >= 3)
        def _():
            k = NK + 2 - s
            slot = lax.rem(s, 2)

            @pl.when(s >= 5)
            def _():
                out_copy(k + 2, slot).wait()
            final(k, slot)
            out_copy(k, slot).start()
        return 0
    lax.fori_loop(0, NK + 3, step, 0)
    out_copy(1, 1).wait()
    out_copy(0, 0).wait()


def local(u, s, c, rot, skew):
    sk = skew.reshape(1, 128)
    anys = pl.BlockSpec(memory_space=pl.ANY)
    vm = pl.BlockSpec(memory_space=pltpu.VMEM)
    D, V = pltpu.SemaphoreType.DMA, pltpu.VMEM
    state = V(((NK + 2) * PITCH, 128), F32)
    coef = V((2 * NK * PITCH, 128), F32)
    packed = pl.pallas_call(
        exchange,
        out_shape=(state, state, coef, coef, state, state),
        in_specs=[anys] * 4 + [vm],
        out_specs=(vm,) * 6,
        scratch_shapes=[V((2, 2, 128, 1024), F32), V((2, 2, 128, 1024), BF16), V((2, 2, 128, 1024), BF16),
                        V((2, 16, 8, 1024), F32), V((2, 16, 8, 1024), BF16), V((2, 16, 8, 1024), BF16),
                        V((2 * 8 * 128, 128), F32),
                        V((2, 2, 8, 1024), F32), V((2, 17, 8, 1024), BF16),
                        V((2, 2, 8, 1024), F32), V((2, 17, 8, 1024), BF16),
                        V((2, 16, 128, 128), F32), V((2, 16, 128, 128), BF16), V((2, 16, 128, 128), BF16),
                        V((128, 128), F32), V((128, 128), BF16), V((128, 128), BF16), V((2, 3, 8, 128), F32),
                        V((2, 64, 128), F32), V((2, 64, 128), BF16), V((2, 64, 128), BF16),
                        V((2, 64, 128), F32), V((2, 64, 128), BF16), V((2, 64, 128), BF16), V((2, 2, 3, 8, 128), F32),
                        V((16, 8192), BF16), V((16, 8192), BF16), V((8, 9, 16, 128), BF16),
                        V((9, 128, 128), BF16), V((2, 9, 16, 128), BF16),
                        D((3, 2)), D((3, 2)), D((3, 2)), D((2,)), D((7,)), D((7,)), D((7,)), D((7,)), D((2, 3)), D((2, 3)),
                        D((2, 2)), D((2, 2)), D((2, 2)), D((2, 2)), D((8,)), D((2,))],
        compiler_params=pltpu.CompilerParams(collective_id=0, has_side_effects=True, vmem_limit_bytes=LIMIT),
        name="exchange",
    )(u, s, c, rot, sk)
    out, _, _ = pl.pallas_call(
        relax,
        out_shape=(jax.ShapeDtypeStruct((16, 128, 1024), F32), state, state),
        in_specs=[vm] * 6,
        out_specs=(anys, vm, vm),
        scratch_shapes=[state, V((2, 2, 128, 1024), F32), D((2,))],
        input_output_aliases={4: 1, 5: 2},
        compiler_params=pltpu.CompilerParams(vmem_limit_bytes=LIMIT),
        name="relax",
    )(*[pltpu.with_memory_space_constraint(x, pltpu.VMEM) for x in packed])
    return out


def solution(mesh):
    placed = (P(None, "ta", "az"), P(None, "ta", "az"), P(None, "ta", "az"), P("ta", "az"), P("ta"))
    return jax.shard_map(
        local, mesh=mesh, in_specs=placed, out_specs=P(None, "ta", "az"), check_vma=False
    )
```

```python
import jax
import jax.numpy as jnp
from jax import lax
from jax.experimental import pallas as pl
from jax.experimental.pallas import tpu as pltpu
from jax.sharding import PartitionSpec as P

F32, BF16 = jnp.float32, jnp.bfloat16
MESH = pl.DeviceIdType.MESH
NAZ, NTA = 8, 16
NK, NJ, ROWS, T0 = 8, 9, 152, 12
PITCH = NJ * ROWS
SIXTY = 1.0 / 48.0
LIMIT = 16100 * 1024
RED_ROWS = ((3, 4, 5, 6, 7), (0, 1, 2, 3, 4))
BLACK_ROWS = ((7, 6, 5, 4), (0, 1, 2, 3))
COEF_ROWS = (((5, 0), (6, 0), (7, 0), (6, 1), (7, 1)), ((0, 0), (1, 0), (2, 0), (0, 1), (1, 1)))


def row(kk, j, rho):
    return kk * PITCH + j * ROWS + rho


def sweep(fn, top, bottom):
    def one(i, _):
        fn(top - i)
        return 0
    lax.fori_loop(0, top - bottom + 1, one, 0)


def half(k, colour, src, own, sg, jg, rho, nj, emit):
    rowi = lax.broadcasted_iota(jnp.int32, (8, 128), 0)
    lane = lax.broadcasted_iota(jnp.int32, (8, 128), 1)
    odd = ((rowi + lane) & 1) == 1
    first, last = lane == 0, lane == 127
    st = (k + 1) * PITCH
    co = (k + colour * NK) * PITCH
    cen = [src[pl.ds(st + j * ROWS + rho, 8), :] for j in range(NJ)]
    rl = [pltpu.roll(x, 1, 1) for x in cen]
    rr = [pltpu.roll(x, 127, 1) for x in cen]
    for j in range(nj):
        off = j * ROWS + rho
        left = jnp.where(first, rl[(j - 1) % NJ], rl[j])
        right = jnp.where(last, rr[(j + 1) % NJ], rr[j])
        lo, hi = src[pl.ds(st - PITCH + off, 8), :], src[pl.ds(st + PITCH + off, 8), :]
        rad = jnp.where(odd, hi, lo) if colour == 0 else jnp.where(odd, lo, hi)
        d1 = src[pl.ds(st + off + 1, 8), :] - src[pl.ds(st + off - 1, 8), :]
        d2 = own[pl.ds(st + off + 2, 8), :] - own[pl.ds(st + off - 2, 8), :]
        acc = ((jg[pl.ds(co + off, 8), :] + rad) + cen[j]) + (left + right)
        emit(j, rho, acc * 0.25 - sg[pl.ds(co + off, 8), :] * (d1 * 8.0 - d2))


def update(k, colour, src, own, dst, sg, jg, tiles):
    st = (k + 1) * PITCH

    def emit(j, rho, val):
        dst[pl.ds(st + j * ROWS + rho, 8), :] = val
    for i in tiles:
        half(k, colour, src, own, sg, jg, 8 + 8 * i, NJ, emit)


def exchange(u_hbm, s_hbm, c_hbm, rot_hbm, sk, r_a, b_a, sg, jg, r_b, b_b,
             us, ss, cs, eu, es, ec, er, su, tb, hu, hb, ku, ks, kc, pu, ps, pc, pd, fu, fs, fc, qu, qs, qc, qd,
             w0, w1, v, cyc, cych,
             in_sem, edge_sem, col_sem, own_sem, p1s, p1r, p3s, p3r, azs, azr, tas, tar, dis, dir_, cys, cyr):
    az, ta = lax.axis_index("az"), lax.axis_index("ta")
    up, down = lax.rem(ta + NTA - 1, NTA), lax.rem(ta + 1, NTA)
    left_az, right_az = lax.rem(az + NAZ - 1, NAZ), lax.rem(az + 1, NAZ)
    others = [lax.rem(az + o, NAZ) for o in range(1, NAZ)]
    diagonals = [(side, other, t, a) for side, t in ((0, down), (1, up)) for other, a in ((0, right_az), (1, left_az))]

    rowi = lax.broadcasted_iota(jnp.int32, (8, 128), 0)
    lane = lax.broadcasted_iota(jnp.int32, (8, 128), 1)
    odd = ((rowi + lane) & 1) == 1
    lane16 = lax.broadcasted_iota(jnp.int32, (16, 128), 1)
    row16 = lax.broadcasted_iota(jnp.int32, (16, 128), 0)
    odd16 = ((lane16 + row16) & 1) == 1
    low16 = lane16 < 64

    def remote(src, dst, ssem, rsem, dev):
        return pltpu.make_async_remote_copy(src_ref=src, dst_ref=dst, send_sem=ssem, recv_sem=rsem,
                                            device_id=dev, device_id_type=MESH)

    def in_copies(k, slot):
        pair = pl.ds(2 * k, 2)
        return [pltpu.make_async_copy(h.at[pair], dst.at[slot], in_sem.at[i, slot])
                for i, (h, dst) in enumerate(((u_hbm, us), (s_hbm, ss), (c_hbm, cs)))]

    edges = [pltpu.make_async_copy(h.at[:, pl.ds(t, 8), :], e.at[side], edge_sem.at[q, side])
             for q, (h, e) in enumerate(((u_hbm, eu), (s_hbm, es), (c_hbm, ec))) for side, t in ((0, 120), (1, 0))]
    cols = [pltpu.make_async_copy(h.at[:, :, pl.ds(n, 128)], e.at[side], col_sem.at[q, side])
            for q, (h, e) in enumerate(((u_hbm, ku), (s_hbm, ks), (c_hbm, kc))) for side, n in ((0, 0), (1, 896))]

    barrier = pltpu.get_barrier_semaphore()
    for d in others:
        pl.semaphore_signal(barrier, inc=1, device_id={"az": d}, device_id_type=MESH)
    for t in (up, down):
        for a in range(NAZ):
            pl.semaphore_signal(barrier, inc=1, device_id={"ta": t, "az": a}, device_id_type=MESH)
    for c in cols: c.start()
    for c in edges: c.start()
    own = pltpu.make_async_copy(rot_hbm.at[pl.ds(16 * az, 16), :], w0.at[:, pl.ds(1024 * az, 1024)], own_sem.at[0])
    own.start()
    for c in in_copies(NK - 1, 0): c.start()
    for c in in_copies(NK - 2, 1): c.start()
    pl.semaphore_wait(barrier, 3 * NAZ - 1)
    first_hop = [remote(rot_hbm.at[pl.ds(16 * d, 16), :], w0.at[:, pl.ds(1024 * az, 1024)], p1s.at[o], p1r.at[o], {"az": d})
                 for o, d in enumerate(others)]
    for c in first_hop: c.start()

    for c in cols: c.wait()

    def columns(i, _):
        rows = pl.ds(pl.multiple_of(16 * i, 16), 16)
        for src, dst in ((ku, pu), (ks, ps), (kc, pc)):
            acc = jnp.zeros((16, 128), F32)
            for k in range(NK):
                even = jnp.where(low16, src[0, 2 * k, rows, :].astype(F32), src[1, 2 * k, rows, :].astype(F32))
                odd_l = jnp.where(low16, src[0, 2 * k + 1, rows, :].astype(F32), src[1, 2 * k + 1, rows, :].astype(F32))
                red, black = jnp.where(odd16, odd_l, even), jnp.where(odd16, even, odd_l)
                for a, x in ((k, red), (k + 8, black)):
                    acc = jnp.where((lane16 >> 3) == a, pltpu.roll(x, (8 * a + 4) % 128, 1), acc)
            dst[rows, :] = acc.astype(dst.dtype)
        return 0
    lax.fori_loop(0, 8, columns, 0)
    for q, src in enumerate((pu, ps, pc)):
        pd[0, q] = src[112:128, :].astype(F32)[8:]
        pd[1, q] = src[0:16, :].astype(F32)[:8]
    mine16 = (lane16 & 7) < 4
    for src, dst in ((pu, fu), (ps, fs), (pc, fc)):
        for i in range(4):
            early, late = src[16 * i:16 * i + 16, :].astype(F32), src[64 + 16 * i:80 + 16 * i, :].astype(F32)
            dst[0, 16 * i:16 * i + 16, :] = jnp.where(mine16, early, pltpu.roll(late, 4, 1)).astype(dst.dtype)
            dst[1, 16 * i:16 * i + 16, :] = jnp.where(mine16, pltpu.roll(early, 124, 1), late).astype(dst.dtype)
    az_hop = [remote(a.at[side], b.at[side], azs.at[side, q], azr.at[side, q], {"az": d})
              for side, d in ((0, right_az), (1, left_az)) for q, (a, b) in enumerate(((fu, qu), (fs, qs), (fc, qc)))]
    diag_hop = [remote(pd.at[side], qd.at[side, other], dis.at[side, other], dir_.at[side, other], {"ta": t, "az": a})
                for side, other, t, a in diagonals]
    for c in az_hop + diag_hop: c.start()

    for c in edges: c.wait()
    for side in range(2):
        for q, e in enumerate((eu, es, ec)):
            for j in range(8):
                ln = slice(128 * j, 128 * j + 128)
                base = (side * 8 + j) * 128
                for k in range(NK):
                    even, odd_layer = e[side, 2 * k, :, ln].astype(F32), e[side, 2 * k + 1, :, ln].astype(F32)
                    er[base + 8 * k:base + 8 * k + 8, :] = jnp.where(odd, odd_layer, even)
                    er[base + 64 + 8 * k:base + 72 + 8 * k, :] = jnp.where(odd, even, odd_layer)
                if q == 0:
                    for i, t in enumerate(RED_ROWS[side]):
                        tb[side, i, :, ln] = er[pl.ds(base + t, NK, stride=8), :].astype(BF16)
                    for i, t in enumerate(BLACK_ROWS[side]):
                        tile = er[pl.ds(base + 64 + t, NK, stride=8), :]
                        if i < 2:
                            su[side, i, :, ln] = tile
                        else:
                            tb[side, 3 + i, :, ln] = tile.astype(BF16)
                else:
                    for i, (t, colour) in enumerate(COEF_ROWS[side]):
                        tb[side, 2 + 5 * q + i, :, ln] = er[pl.ds(base + 64 * colour + t, NK, stride=8), :].astype(BF16)
    time_hop = [remote(a.at[side], b.at[side], tas.at[side, q], tar.at[side, q], {"ta": d})
                for side, d in ((0, down), (1, up)) for q, (a, b) in enumerate(((su, hu), (tb, hb)))]
    for c in time_hop: c.start()

    def pack(s, _):
        k = NK - 1 - s
        slot = lax.rem(s, 2)
        for c in in_copies(k, slot): c.wait()
        st, c0, c1 = (k + 1) * PITCH, k * PITCH, (k + NK) * PITCH
        for i in range(8):
            rows = slice(16 * i, 16 * i + 16)
            for j in range(8):
                ln = slice(128 * j, 128 * j + 128)
                e16, o16 = ss[slot, 0, rows, ln].astype(F32) * SIXTY, ss[slot, 1, rows, ln].astype(F32) * SIXTY
                f16, p16 = cs[slot, 0, rows, ln].astype(F32), cs[slot, 1, rows, ln].astype(F32)
                for h in range(2):
                    part, r8 = slice(8 * h, 8 * h + 8), slice(16 * i + 8 * h, 16 * i + 8 * h + 8)
                    at = j * ROWS + T0 + 16 * i + 8 * h
                    for e, o, ra, rb, pa, pb in ((us[slot, 0, r8, ln], us[slot, 1, r8, ln], r_a, b_a, st, st),
                                                 (e16[part], o16[part], sg, sg, c0, c1), (f16[part], p16[part], jg, jg, c0, c1)):
                        ra[pl.ds(pa + at, 8), :] = jnp.where(odd, o, e)
                        rb[pl.ds(pb + at, 8), :] = jnp.where(odd, e, o)

        @pl.when(s + 2 < NK)
        def _():
            for c in in_copies(k - 2, slot): c.start()
        return 0

    own.wait()
    for c in first_hop: c.wait_recv()
    here = jnp.where(lane16 == row16 + 16 * az, jnp.broadcast_to(sk[...], (16, 128)).astype(F32), 0.0)
    amount = jnp.broadcast_to(jnp.sum(here, axis=1, keepdims=True).astype(jnp.int32), (16, 128))
    src, dst = w0, w1
    for b in range(6):
        bit = ((amount >> b) & 1) == 1
        for p in range(64):
            f = (p - (1 << b)) % 64
            dst[:, 128 * p:128 * p + 128] = jnp.where(bit, src[:, 128 * f:128 * f + 128], src[:, 128 * p:128 * p + 128])
        src, dst = dst, src
    for d in range(NAZ):
        for jj in range(8):
            v[d, jj] = w0[:, 1024 * d + 128 * jj:1024 * d + 128 * jj + 128]
        after, before = (8 * d + 8) % 64, (8 * d - 1) % 64
        v[d, 8] = jnp.where(low16, w0[:, 128 * after:128 * after + 128], w0[:, 128 * before:128 * before + 128])
    block = pl.ds(16 * az, 16)
    mine = pltpu.make_async_copy(v.at[az], cyc.at[:, block, :], own_sem.at[1])
    mine.start()
    second_hop = [remote(v.at[d], cyc.at[:, block, :], p3s.at[o], p3r.at[o], {"az": d}) for o, d in enumerate(others)]
    for c in second_hop: c.start()
    beyond = [[remote(v.at[d], cych.at[side], cys.at[d], cyr.at[side], {"ta": t, "az": d}) for d in range(NAZ)]
              for side, t in ((0, down), (1, up))]

    lax.fori_loop(0, NK, pack, 0)

    @pl.when(az == NAZ - 1)
    def _():
        for c in beyond[0]: c.start()

    @pl.when(az == 0)
    def _():
        for c in beyond[1]: c.start()

    zero = jnp.zeros((8, 128), F32)
    for j in range(NJ):
        for i in range(ROWS // 8):
            for ref in (b_a, r_b, b_b):
                ref[pl.ds(row(NK + 1, j, 8 * i), 8), :] = zero

    for c in az_hop: c.wait_recv()
    for c in diag_hop: c.wait_recv()
    mine_lane = (lane & 7) < 4

    def place(q, x, rho):
        if q == 1:
            x = x * SIXTY
        for a in range(16):
            y = pltpu.roll(x, (124 - 8 * a) % 128, 1)
            if q == 0:
                (r_a if a < 8 else b_a)[pl.ds(row(a % 8 + 1, NJ - 1, rho), 8), :] = y
            else:
                (sg if q == 1 else jg)[pl.ds(a * PITCH + (NJ - 1) * ROWS + rho, 8), :] = y

    for q, b in enumerate((qu, qs, qc)):
        for side, rho in ((0, T0 - 8), (1, T0 + 128)):
            place(q, jnp.where(mine_lane, qd[side, 0, q], qd[side, 1, q]), rho)
        for i in range(4):
            lt, rt = b[0, 16 * i:16 * i + 16, :].astype(F32), b[1, 16 * i:16 * i + 16, :].astype(F32)
            early = jnp.where(mine16, lt, pltpu.roll(rt, 4, 1))
            late = jnp.where(mine16, pltpu.roll(lt, 124, 1), rt)
            for h in range(2):
                place(q, early[8 * h:8 * h + 8], T0 + 16 * i + 8 * h)
                place(q, late[8 * h:8 * h + 8], T0 + 64 + 16 * i + 8 * h)

    sweep(lambda k: update(k, 0, b_a, r_a, r_b, sg, jg, range(1, 16)), 7, 1)
    sweep(lambda k: update(k, 1, r_b, b_a, b_b, sg, jg, range(2, 15)), 7, 2)

    mine.wait()
    for c in second_hop: c.wait_recv()
    for side in range(2): beyond[side][0].wait_recv()
    for j in range(NJ):
        for i in range(8):
            x = cyc[j, 16 * i:16 * i + 16, :].astype(F32)
            for ref in (b_a, r_b, b_b):
                ref[pl.ds(row(0, j, T0 + 16 * i), 16), :] = x
        top, bottom = cych[0, j].astype(F32)[8:], cych[1, j].astype(F32)[:8]
        for ref in (b_a, r_b, b_b):
            ref[pl.ds(row(0, j, T0 - 8), 8), :] = top
            ref[pl.ds(row(0, j, T0 + 128), 8), :] = bottom

    for c in time_hop: c.wait_recv()

    def spread(ref, base, j, t, tile):
        ref[pl.ds(base + j * ROWS + T0 + t, NK, stride=PITCH), :] = tile

    for j in range(8):
        ln = slice(128 * j, 128 * j + 128)
        for side in range(2):
            shift = -8 if side == 0 else 128
            for i, t in enumerate(RED_ROWS[side]):
                spread(r_a, PITCH, j, t + shift, hb[side, i, :, ln].astype(F32))
            for i, t in enumerate(BLACK_ROWS[side]):
                spread(b_a, PITCH, j, t + shift, hu[side, i, :, ln] if i < 2 else hb[side, 3 + i, :, ln].astype(F32))
            for i, (t, colour) in enumerate(COEF_ROWS[side]):
                spread(sg, colour * NK * PITCH, j, t + shift, hb[side, 7 + i, :, ln].astype(F32) * SIXTY)
                spread(jg, colour * NK * PITCH, j, t + shift, hb[side, 12 + i, :, ln].astype(F32))

    for c in first_hop + second_hop + time_hop + az_hop + diag_hop: c.wait_send()

    @pl.when(az == NAZ - 1)
    def _():
        for c in beyond[0]: c.wait_send()

    @pl.when(az == 0)
    def _():
        for c in beyond[1]: c.wait_send()


def relax(r_0, b_0, sg, jg, _r, _b, out_hbm, r_1, b_1, r_2, outs, out_sem):
    rowi = lax.broadcasted_iota(jnp.int32, (8, 128), 0)
    lane = lax.broadcasted_iota(jnp.int32, (8, 128), 1)
    odd = ((rowi + lane) & 1) == 1

    def out_copy(k, slot):
        return pltpu.make_async_copy(outs.at[slot], out_hbm.at[pl.ds(2 * k, 2)], out_sem.at[slot])

    zero = jnp.zeros((8, 128), F32)
    for j in range(NJ):
        for i in range(ROWS // 8):
            r_2[pl.ds(row(NK + 1, j, 8 * i), 8), :] = zero
            r_2[pl.ds(row(0, j, 8 * i), 8), :] = b_0[pl.ds(row(0, j, 8 * i), 8), :]

    def final(k, slot):
        st = (k + 1) * PITCH

        def emit(j, rho, val):
            red = r_2[pl.ds(st + j * ROWS + rho, 8), :]
            t = rho - T0
            outs[slot, 0, t:t + 8, 128 * j:128 * j + 128] = jnp.where(odd, val, red)
            outs[slot, 1, t:t + 8, 128 * j:128 * j + 128] = jnp.where(odd, red, val)
        for i in range(16):
            half(k, 1, r_2, b_1, sg, jg, T0 + 8 * i, 8, emit)

    edge_0, edge_1 = (0, 16), (0, 1, 15, 16)

    def step(s, _):
        @pl.when(s < NK - 1)
        def _():
            update(NK - 1 - s, 0, b_0, r_0, r_1, sg, jg, edge_0)

        @pl.when(s == NK - 1)
        def _():
            update(0, 0, b_0, r_0, r_1, sg, jg, range(17))

        @pl.when((s >= 1) & (s < NK - 1))
        def _():
            update(NK - s, 1, r_1, b_0, b_1, sg, jg, edge_1)

        @pl.when((s >= NK - 1) & (s < NK + 1))
        def _():
            update(NK - s, 1, r_1, b_0, b_1, sg, jg, range(17))

        @pl.when((s >= 2) & (s < NK + 2))
        def _():
            update(NK + 1 - s, 0, b_1, r_1, r_2, sg, jg, range(17))

        @pl.when(s >= 3)
        def _():
            k = NK + 2 - s
            slot = lax.rem(s, 2)

            @pl.when(s >= 5)
            def _():
                out_copy(k + 2, slot).wait()
            final(k, slot)
            out_copy(k, slot).start()
        return 0
    lax.fori_loop(0, NK + 3, step, 0)
    out_copy(1, 1).wait()
    out_copy(0, 0).wait()


def local(u, s, c, rot, skew):
    sk = skew.reshape(1, 128)
    anys = pl.BlockSpec(memory_space=pl.ANY)
    vm = pl.BlockSpec(memory_space=pltpu.VMEM)
    D, V = pltpu.SemaphoreType.DMA, pltpu.VMEM
    state = V(((NK + 2) * PITCH, 128), F32)
    coef = V((2 * NK * PITCH, 128), F32)
    packed = pl.pallas_call(
        exchange,
        out_shape=(state, state, coef, coef, state, state),
        in_specs=[anys] * 4 + [vm],
        out_specs=(vm,) * 6,
        scratch_shapes=[V((2, 2, 128, 1024), F32), V((2, 2, 128, 1024), BF16), V((2, 2, 128, 1024), BF16),
                        V((2, 16, 8, 1024), F32), V((2, 16, 8, 1024), BF16), V((2, 16, 8, 1024), BF16),
                        V((2 * 8 * 128, 128), F32),
                        V((2, 2, 8, 1024), F32), V((2, 17, 8, 1024), BF16),
                        V((2, 2, 8, 1024), F32), V((2, 17, 8, 1024), BF16),
                        V((2, 16, 128, 128), F32), V((2, 16, 128, 128), BF16), V((2, 16, 128, 128), BF16),
                        V((128, 128), F32), V((128, 128), BF16), V((128, 128), BF16), V((2, 3, 8, 128), F32),
                        V((2, 64, 128), F32), V((2, 64, 128), BF16), V((2, 64, 128), BF16),
                        V((2, 64, 128), F32), V((2, 64, 128), BF16), V((2, 64, 128), BF16), V((2, 2, 3, 8, 128), F32),
                        V((16, 8192), BF16), V((16, 8192), BF16), V((8, 9, 16, 128), BF16),
                        V((9, 128, 128), BF16), V((2, 9, 16, 128), BF16),
                        D((3, 2)), D((3, 2)), D((3, 2)), D((2,)), D((7,)), D((7,)), D((7,)), D((7,)), D((2, 3)), D((2, 3)),
                        D((2, 2)), D((2, 2)), D((2, 2)), D((2, 2)), D((8,)), D((2,))],
        compiler_params=pltpu.CompilerParams(collective_id=0, has_side_effects=True, vmem_limit_bytes=LIMIT),
        name="exchange",
    )(u, s, c, rot, sk)
    out, _, _ = pl.pallas_call(
        relax,
        out_shape=(jax.ShapeDtypeStruct((16, 128, 1024), F32), state, state),
        in_specs=[vm] * 6,
        out_specs=(anys, vm, vm),
        scratch_shapes=[state, V((2, 2, 128, 1024), F32), D((2,))],
        input_output_aliases={4: 1, 5: 2},
        compiler_params=pltpu.CompilerParams(vmem_limit_bytes=LIMIT),
        name="relax",
    )(*[pltpu.with_memory_space_constraint(x, pltpu.VMEM) for x in packed])
    return out


def solution(mesh):
    placed = (P(None, "ta", "az"), P(None, "ta", "az"), P(None, "ta", "az"), P("ta", "az"), P("ta"))
    return jax.shard_map(
        local, mesh=mesh, in_specs=placed, out_specs=P(None, "ta", "az"), check_vma=False
    )
```
